256 devices in a mesh: chan: 16 (over x_lo, y, core), pulse: 16 (over x_hi, z).
Axes of the slice: x: 4 (x_hi: 2, x_lo: 2; x = x_hi * 2 + x_lo), y: 4, z: 8, core: 2. Of those that a mesh axis runs over, the one named last changes fastest.
Arguments:
- echoes: float32 [16, 2, 4096, 4096], P('chan', None, 'pulse'), may hold values from -6 to 6
- chirp_phase: float32 [4096], replicated, may hold values from -3.140625 to 3.140625
- rcmc_kernel: float32 [32, 128, 128], P('pulse'), may hold values from -0.5 to 0.5
- rcmc_offset: int32 [32], P('pulse'), may hold values from 1 to 64, as said below
- az_phase: float32 [4096, 32], P(None, 'pulse'), may hold values from -3.140625 to 3.140625
- weight_table: float32 [2, 64], replicated, may hold values from -1.5 to 1.5
- weight_index: int32 [16, 32], P('chan'), may hold values from 0 to 63
Outputs:
- image: float32 [2, 4096, 4096], P(None, 'chan', 'pulse')
The draws below stay inside these ranges and needn't reach their ends.
Inputs may be any that keep to these rules, and one draw needn't show every extreme that they name: `rcmc_offset`: every offset is at least 1, and in every draw some block's offset equals 64.
All inputs are finite; a program needn't handle non-finite values.
Results may differ from the reference program's by a relative error of at most 0.0001.
Values sent between devices are 32-bit elements; how exact they have to be, the bound alone decides.
No kernel may reach another device: no remote copies, remote signals or barrier semaphores. Data moves between devices by JAX's collectives and lax.ppermute only.
A program may use at most 128 MiB of HBM per device.

```python
import jax
import jax.numpy as jnp
from jax import lax

PULSES = 4096
GATES = 4096
BLOCK = 128
DBLOCK = 128
TABLE = 64
CHAN = 16
HALF = 64
NBLK = 32
NDBLK = 32


def draw_rcmc_offset(key, part):
    first_key, second_key = jax.random.split(jax.random.fold_in(key, 17))
    offsets_drawn = jax.random.randint(first_key, (NBLK,), 1, HALF + 1)
    forced_spot = jax.random.randint(second_key, (), 0, NBLK)
    return jnp.where(jnp.arange(NBLK) == forced_spot, HALF, offsets_drawn).astype(jnp.int32)


def set_ends(drawn, own_key, least, high):
    index_at = [jax.random.randint(jax.random.fold_in(own_key, axis), (), 0, length) for axis, length in enumerate(drawn.shape)]
    main_axis = drawn.shape.index(max(drawn.shape))
    neighbour = index_at[:main_axis] + [(index_at[main_axis] + 1) % drawn.shape[main_axis]] + index_at[main_axis + 1:]
    return drawn.at[tuple(index_at)].set(least).at[tuple(neighbour)].set(high)


def level_of(key, shape, shards, smallest, high):
    loudness = 1.0
    for axis_at, parts in shards:
        heights = jax.random.uniform(jax.random.fold_in(jax.random.fold_in(key, 6), axis_at), (parts,), jnp.float32, smallest / len(shards), high / len(shards))
        loudness = loudness * jnp.repeat(jnp.exp(heights), shape[axis_at] // parts).reshape((-1,) + (1,) * (len(shape) - 1 - axis_at))
    return loudness


def gaussian(rng, shape, scale, limit, cuts=(), held_as=jnp.bfloat16):
    gain = level_of(rng, shape, cuts, -0.22, 0.18) if cuts else 1.0
    array = jax.random.normal(rng, shape, jnp.float32) * scale * gain
    return jnp.minimum(jnp.maximum(array, -limit), limit).astype(held_as)


def setup_inputs(seed: int = 0) -> dict:
    keys = jax.random.split(jax.random.key(seed), 8)
    return {
        "echoes": gaussian(keys[0], (CHAN, 2, PULSES, GATES), 1.0, 6.0, ((0, 16), (2, 16)), jnp.float32),
        "chirp_phase": jnp.clip(jax.random.uniform(keys[1], (GATES,), jnp.float32, -3.140625, 3.140625), -3.140625, 3.140625),
        "rcmc_kernel": gaussian(keys[2], (NBLK, BLOCK, BLOCK), BLOCK ** -0.5, 0.5, ((0, 16),), jnp.float32),
        "rcmc_offset": draw_rcmc_offset(jax.random.fold_in(keys[7], 71), 0),
        "az_phase": jnp.clip(jax.random.uniform(keys[4], (PULSES, NBLK), jnp.float32, -3.140625, 3.140625), -3.140625, 3.140625),
        "weight_table": gaussian(keys[5], (2, TABLE), 0.25, 1.5, (), jnp.float32),
        "weight_index": set_ends(jax.random.randint(keys[6], (CHAN, NDBLK), 0, TABLE), jax.random.fold_in(keys[6], 1), 0, TABLE - 1).astype(jnp.int32),
    }


def channel_image(channel_echo, index_row, chirp_phase, rcmc_kernel, rcmc_offset, az_phase, weight_table):
    signal = lax.complex(channel_echo[0], channel_echo[1])
    spectrum = jnp.fft.fft(signal, axis=1, norm="ortho")
    chirp = lax.complex(jnp.cos(chirp_phase), jnp.sin(chirp_phase))
    compressed = jnp.fft.ifft(spectrum * chirp[None, :], axis=1, norm="ortho")
    doppler = jnp.fft.fft(compressed, axis=0, norm="ortho")
    padded = jnp.pad(doppler, ((0, 0), (0, HALF)))
    starts = jnp.arange(NBLK, dtype=jnp.int32) * BLOCK + rcmc_offset.astype(jnp.int32)
    gather_index = (starts[:, None] + jnp.arange(BLOCK, dtype=jnp.int32)[None, :]).reshape(-1)
    windows = jnp.take(padded, gather_index, axis=1).reshape(PULSES, NBLK, BLOCK)
    mig_re = jnp.einsum("pbj,bji->pbi", jnp.real(windows), rcmc_kernel, precision=lax.Precision.HIGHEST)
    mig_im = jnp.einsum("pbj,bji->pbi", jnp.imag(windows), rcmc_kernel, precision=lax.Precision.HIGHEST)
    migrated = lax.complex(mig_re, mig_im).reshape(PULSES, GATES)
    phase_factor = jnp.repeat(lax.complex(jnp.cos(az_phase), jnp.sin(az_phase)), BLOCK, axis=1)
    weights = lax.complex(weight_table[0, index_row], weight_table[1, index_row])
    weight_full = jnp.repeat(weights, DBLOCK)[:, None]
    filtered = migrated * phase_factor * weight_full
    focused = jnp.fft.ifft(filtered, axis=0, norm="ortho")
    return jnp.stack([jnp.real(focused), jnp.imag(focused)])


def reference(echoes, chirp_phase, rcmc_kernel, rcmc_offset, az_phase, weight_table, weight_index):
    def add_channel(running, scan_item):
        channel_echo, index_row = scan_item
        term = channel_image(channel_echo, index_row, chirp_phase, rcmc_kernel, rcmc_offset, az_phase, weight_table)
        return running + term, None

    start_value = jnp.zeros((2, PULSES, GATES), jnp.float32)
    running, _ = lax.scan(add_channel, start_value, (echoes, weight_index))
    return running
```

```python
import functools
import math

import jax
import jax.numpy as jnp
import numpy as np
from jax import lax
from jax.experimental import pallas as pl
from jax.experimental.pallas import tpu as pltpu
from jax.sharding import PartitionSpec as P

BLOCK = 128
DBLOCK = 128
SLABS = 32
INNER = 128
ROWS = 32


def split(values):
    high = values.astype(jnp.bfloat16)
    low = (values - high.astype(jnp.float32)).astype(jnp.bfloat16)
    return high, low


def dot(left, right):
    return jnp.dot(left, right, preferred_element_type=jnp.float32)


def dot3(left, right):
    return dot(left[0], right[0]) + dot(left[0], right[1]) + dot(left[1], right[0])


def inner_tables():
    index = np.arange(INNER)
    angles = 2.0 * math.pi / INNER * (index[:, None] * index[None, :] % INNER)
    table = np.block([[np.cos(angles), -np.sin(angles)], [np.sin(angles), np.cos(angles)]])
    bf16 = jnp.bfloat16.dtype
    high = table.astype(np.float32).astype(bf16)
    low = (table - high.astype(np.float64)).astype(np.float32).astype(bf16)
    return np.stack([high, low]), np.stack([high.T, low.T])


def twiddles():
    length = SLABS * INNER
    angles = 2.0 * math.pi / length * (np.arange(SLABS)[:, None] * np.arange(INNER)[None, :])
    return np.stack([np.cos(angles), -np.sin(angles)]).astype(np.float32)


def rotate(value, turn, length, sign):
    re, im = value
    if turn == 0:
        return value
    if 4 * turn == length:
        return (-im, re) if sign > 0 else (im, -re)
    half = math.sqrt(0.5)
    if 8 * turn == length:
        return ((re - im) * half, (re + im) * half) if sign > 0 else ((re + im) * half, (im - re) * half)
    if 8 * turn == 3 * length:
        return ((-re - im) * half, (re - im) * half) if sign > 0 else ((im - re) * half, (-re - im) * half)
    cosine = math.cos(2.0 * math.pi * turn / length)
    sine = sign * math.sin(2.0 * math.pi * turn / length)
    return re * cosine - im * sine, re * sine + im * cosine


def butterflies(values, sign):
    length = len(values)
    if length == 1:
        return values
    even = butterflies(values[0::2], sign)
    odd = butterflies(values[1::2], sign)
    lower, upper = [], []
    for turn in range(length // 2):
        er, ei = even[turn]
        tr, ti = rotate(odd[turn], turn, length, sign)
        lower.append((er + tr, ei + ti))
        upper.append((er - tr, ei - ti))
    return lower + upper


def times(re, im, cr, ci):
    return re * cr - im * ci, re * ci + im * cr


def range_kernel(offset_ref, x_ref, fwd_ref, inv_ref, tw_ref, chirp_ref, *refs):
    z0_ref, z1_ref, mid_ref, y_ref = refs[-4:]

    def first(tile, carry):
        rows = pl.ds(pl.multiple_of(tile * 8, 8), 8)
        values = [
            (x_ref[0, 0, rows, a * INNER : (a + 1) * INNER], x_ref[0, 1, rows, a * INNER : (a + 1) * INNER])
            for a in range(SLABS)
        ]
        for k, (re, im) in enumerate(butterflies(values, -1)):
            re, im = times(re, im, tw_ref[0, k : k + 1, :], tw_ref[1, k : k + 1, :])
            mid_ref[k, rows, :INNER] = re
            mid_ref[k, rows, INNER:] = im
        return carry

    lax.fori_loop(0, ROWS // 8, first, 0)

    group = 256 // ROWS
    chains = 2

    def middle(step, carry):
        spans = [pl.ds(pl.multiple_of((step * chains + c) * group, group), group) for c in range(chains)]
        spectra = [dot3(split(mid_ref[ks].reshape(256, 2 * INNER)), (fwd_ref[0], fwd_ref[1])) for ks in spans]
        for ks, spec in zip(spans, spectra):
            spec = spec.reshape(group, ROWS, 2 * INNER)
            cr = chirp_ref[0, ks, :].reshape(group, 1, INNER)
            ci = chirp_ref[1, ks, :].reshape(group, 1, INNER)
            re, im = times(spec[:, :, :INNER], spec[:, :, INNER:], cr, ci)
            filtered = jnp.concatenate([re, im], axis=2).reshape(256, 2 * INNER)
            back = dot3(split(filtered), (inv_ref[0], inv_ref[1])).reshape(group, ROWS, 2 * INNER)
            tr = tw_ref[0, ks, :].reshape(group, 1, INNER)
            ti = tw_ref[1, ks, :].reshape(group, 1, INNER)
            re, im = times(back[:, :, :INNER], back[:, :, INNER:], tr, -ti)
            mid_ref[ks, :, :INNER] = re
            mid_ref[ks, :, INNER:] = im
        return carry

    lax.fori_loop(0, SLABS // (group * chains), middle, 0)

    def last(tile, carry):
        rows = pl.ds(pl.multiple_of(tile * 8, 8), 8)
        lower = pl.ds(pl.multiple_of(ROWS + tile * 8, 8), 8)
        values = [(mid_ref[k, rows, :INNER], mid_ref[k, rows, INNER:]) for k in range(SLABS)]
        for a, (re, im) in enumerate(butterflies(values, 1)):
            y_ref[a, rows, :] = re
            y_ref[a, lower, :] = im
        return carry

    lax.fori_loop(0, ROWS // 8, last, 0)
    y_ref[SLABS] = jnp.zeros((2 * ROWS, INNER), jnp.float32)
    lanes = lax.broadcasted_iota(jnp.int32, (2 * ROWS, INNER), 1)

    def window(step, carry):
        for part in range(4):
            dest = step * 4 + part
            for block, z_ref in ((0, z0_ref), (1, z1_ref)):
                slab = 2 * dest + block
                back = INNER - offset_ref[slab]
                here = pltpu.roll(y_ref[slab], back, 1)
                after = pltpu.roll(y_ref[slab + 1], back, 1)
                shifted = jnp.where(lanes < back, here, after).reshape(2, ROWS, INNER)
                if block:
                    z_ref[dest, 0] = shifted
                else:
                    z_ref[dest] = shifted
        return carry

    lax.fori_loop(0, SLABS // 8, window, 0)


def range_compress(half, offsets, echoes, fwd, inv, chirp, other=None):
    pulses, gates = echoes.shape[2] // 2, echoes.shape[3]
    dests = gates // (2 * BLOCK)
    steps = pulses // ROWS
    outs = [
        jax.ShapeDtypeStruct((dests, 2, pulses, BLOCK), jnp.float32),
        jax.ShapeDtypeStruct((dests, 2, 2, pulses, BLOCK), jnp.float32),
    ]
    whole3 = pl.BlockSpec((2, 2 * INNER, 2 * INNER), lambda i, *_: (0, 0, 0))
    table = pl.BlockSpec((2, SLABS, INNER), lambda i, *_: (0, 0, 0))
    in_specs = [pl.BlockSpec((1, 2, ROWS, gates), lambda i, *_: (0, 0, half * steps + i, 0)), whole3, whole3, table, table]
    args = [offsets, echoes, fwd, inv, jnp.asarray(twiddles()), chirp]
    aliases = {}
    if other is not None:
        in_specs.append(pl.BlockSpec(memory_space=pl.ANY))
        aliases = {len(args): 1}
        args.append(other)
    return pl.pallas_call(
        range_kernel,
        grid_spec=pltpu.PrefetchScalarGridSpec(
            num_scalar_prefetch=1,
            grid=(steps,),
            in_specs=in_specs,
            out_specs=[
                pl.BlockSpec((dests, 2, ROWS, BLOCK), lambda i, *_: (0, 0, i, 0)),
                pl.BlockSpec((dests, 1, 2, ROWS, BLOCK), lambda i, *_: (0, half, 0, i, 0)),
            ],
            scratch_shapes=[
                pltpu.VMEM((SLABS, ROWS, 2 * INNER), jnp.float32),
                pltpu.VMEM((SLABS + 1, 2 * ROWS, INNER), jnp.float32),
            ],
        ),
        out_shape=outs,
        input_output_aliases=aliases,
        name="range_compress",
    )(*args)


def azimuth_kernel(count, *refs):
    x_refs = refs[:count]
    fwd_ref, inv_ref, tw_ref, gain_ref, o_ref, mid_ref, wide_ref = refs[count:]

    def slab(a, part, rows):
        if count == 2:
            return x_refs[a % 2][a // 2, part, rows, :]
        return x_refs[0][a // 2, a % 2, part, rows, :]

    def first(tile, carry):
        start = pl.multiple_of(tile * 8, 8)
        rows = pl.ds(start, 8)
        lower = pl.ds(pl.multiple_of(INNER + tile * 8, 8), 8)
        values = [(slab(a, 0, rows), slab(a, 1, rows)) for a in range(SLABS)]
        tr, ti = tw_ref[0, rows, :], tw_ref[1, rows, :]
        gr, gi = gain_ref[0, rows, :], gain_ref[1, rows, :]
        for k, (re, im) in enumerate(butterflies(values, -1)):
            re, im = times(re, im, tr[:, k : k + 1], ti[:, k : k + 1])
            lane = slice((k % 2) * INNER, (k % 2 + 1) * INNER)
            mid_ref[k // 2, rows, lane] = re
            mid_ref[k // 2, lower, lane] = im
            wide_ref[k // 2, rows, lane] = jnp.broadcast_to(gr[:, k : k + 1], (8, INNER))
            wide_ref[k // 2, lower, lane] = jnp.broadcast_to(gi[:, k : k + 1], (8, INNER))
        return carry

    lax.fori_loop(0, INNER // 8, first, 0)

    def middle(step, carry):
        pairs = [2 * step, 2 * step + 1]
        spectra = [dot3((inv_ref[0], inv_ref[1]), split(mid_ref[pair])) for pair in pairs]
        for pair, spec in zip(pairs, spectra):
            re, im = times(spec[:INNER], spec[INNER:], wide_ref[pair, :INNER, :], wide_ref[pair, INNER:, :])
            mid_ref[pair] = dot3((fwd_ref[0], fwd_ref[1]), split(jnp.concatenate([re, im], axis=0)))
        return carry

    lax.fori_loop(0, SLABS // 4, middle, 0)

    def last(tile, carry):
        rows = pl.ds(pl.multiple_of(tile * 8, 8), 8)
        lower = pl.ds(pl.multiple_of(INNER + tile * 8, 8), 8)
        halves = (rows, lower)
        tr, ti = tw_ref[0, rows, :], tw_ref[1, rows, :]
        values = []
        for k in range(SLABS):
            lane = slice((k % 2) * INNER, (k % 2 + 1) * INNER)
            re, im = mid_ref[k // 2, rows, lane], mid_ref[k // 2, lower, lane]
            values.append(times(re, im, tr[:, k : k + 1], -ti[:, k : k + 1]))
        for a, (re, im) in enumerate(butterflies(values, 1)):
            o_ref[a // 2, 0, halves[a % 2], :] = re
            o_ref[a // 2, 1, halves[a % 2], :] = im
        return carry

    lax.fori_loop(0, INNER // 8, last, 0)


def azimuth_filter(received, fwd, inv, gain):
    vmem = pl.BlockSpec(memory_space=pltpu.VMEM)
    count = len(received)
    devices = received[0].shape[0]
    return pl.pallas_call(
        functools.partial(azimuth_kernel, count),
        in_specs=[vmem] * (count + 4),
        out_specs=vmem,
        out_shape=jax.ShapeDtypeStruct((devices, 2, 2 * INNER, BLOCK), jnp.float32),
        scratch_shapes=[
            pltpu.VMEM((SLABS // 2, 2 * INNER, 2 * INNER), jnp.float32),
            pltpu.VMEM((SLABS // 2, 2 * INNER, 2 * INNER), jnp.float32),
        ],
        name="azimuth_filter",
    )(*received, fwd, inv, jnp.asarray(twiddles().transpose(0, 2, 1)), gain)


def migrate_kernel(s_ref, kernel_ref, *refs):
    rows = jnp.sum(s_ref[...], axis=0).reshape(-1, BLOCK)
    moved = jnp.dot(rows, kernel_ref[0], precision=lax.Precision.HIGHEST, preferred_element_type=jnp.float32)
    refs[-1][...] = moved.reshape(2, -1, BLOCK)


def migrate(block, parts, kernel, other=None):
    devices, _, pulses, _ = parts.shape
    args = [parts, kernel]
    in_specs = [
        pl.BlockSpec((devices, 2, pulses, BLOCK), lambda i: (0, 0, 0, 0)),
        pl.BlockSpec((1, BLOCK, BLOCK), lambda i: (block, 0, 0)),
    ]
    aliases = {}
    if other is not None:
        in_specs.append(pl.BlockSpec(memory_space=pl.ANY))
        aliases = {2: 0}
        args.append(other)
    return pl.pallas_call(
        migrate_kernel,
        grid=(1,),
        in_specs=in_specs,
        out_specs=pl.BlockSpec((2, pulses, BLOCK), lambda i: (0, 0, block)),
        out_shape=jax.ShapeDtypeStruct((2, pulses, 2 * BLOCK), jnp.float32),
        input_output_aliases=aliases,
        name="migrate",
    )(*args)


def turn(blocks, axis):
    return lax.all_to_all(blocks, axis, split_axis=0, concat_axis=0, tiled=True)


def body(echoes, chirp_phase, rcmc_kernel, rcmc_offset, az_phase, weight_table, weight_index):
    exact = lax.Precision.HIGHEST
    gates = echoes.shape[3]
    pulses = az_phase.shape[0]
    fwd_np, inv_np = inner_tables()
    fwd, inv = jnp.asarray(fwd_np), jnp.asarray(inv_np)
    devices = lax.axis_size("pulse")
    offsets = turn(jnp.broadcast_to(rcmc_offset, (devices, rcmc_offset.shape[0])), "pulse").reshape(-1)
    by_slab = chirp_phase.reshape(INNER, SLABS).T
    chirp = jnp.stack([jnp.cos(by_slab), jnp.sin(by_slab)]) * (1.0 / gates)
    early, partial = range_compress(0, offsets, echoes, fwd, inv, chirp)
    late, full = range_compress(1, offsets, echoes, fwd, inv, chirp, partial)

    table_count = weight_table.shape[1]
    entry_ids = lax.broadcasted_iota(jnp.int32, (weight_index.shape[1], table_count), 1)
    one_hot = (weight_index[0][:, None] == entry_ids).astype(jnp.float32)
    chosen = jnp.dot(weight_table, one_hot.T, precision=exact) * (1.0 / pulses)
    weights = jnp.repeat(chosen, DBLOCK, axis=1)
    phases = az_phase.T
    gain = jnp.stack(times(jnp.cos(phases), jnp.sin(phases), weights[0:1], weights[1:2]))
    gain = gain.reshape(2, 2, INNER, SLABS)

    early = turn(early, "pulse")
    late = turn(late, "pulse")
    full = turn(full, "pulse")
    first = azimuth_filter([early, late], fwd, inv, gain[:, 0])
    first = lax.psum_scatter(first, "chan", scatter_dimension=0, tiled=True)
    image = migrate(0, first, rcmc_kernel)
    second = azimuth_filter([full], fwd, inv, gain[:, 1])
    second = turn(second, "chan")
    return migrate(1, second, rcmc_kernel, image)


def solution(mesh):
    return jax.shard_map(
        body,
        mesh=mesh,
        in_specs=(
            P("chan", None, "pulse", None),
            P(),
            P("pulse", None, None),
            P("pulse"),
            P(None, "pulse"),
            P(),
            P("chan", None),
        ),
        out_specs=P(None, "chan", "pulse"),
        check_vma=False,
    )
```

```python
import functools
import math

import jax
import jax.numpy as jnp
import numpy as np
from jax import lax
from jax.experimental import pallas as pl
from jax.experimental.pallas import tpu as pltpu
from jax.sharding import PartitionSpec as P

BLOCK = 128
DBLOCK = 128
SLABS = 32
INNER = 128
ROWS = 32
EARLY = 2


def split(values):
    high = values.astype(jnp.bfloat16)
    low = (values - high.astype(jnp.float32)).astype(jnp.bfloat16)
    return high, low


def dot(left, right):
    return jnp.dot(left, right, preferred_element_type=jnp.float32)


def dot3(left, right):
    return dot(left[0], right[0]) + dot(left[0], right[1]) + dot(left[1], right[0])


def inner_tables():
    index = np.arange(INNER)
    angles = 2.0 * math.pi / INNER * (index[:, None] * index[None, :] % INNER)
    table = np.block([[np.cos(angles), -np.sin(angles)], [np.sin(angles), np.cos(angles)]])
    bf16 = jnp.bfloat16.dtype
    high = table.astype(np.float32).astype(bf16)
    low = (table - high.astype(np.float64)).astype(np.float32).astype(bf16)
    return np.stack([high, low]), np.stack([high.T, low.T])


def twiddles():
    length = SLABS * INNER
    angles = 2.0 * math.pi / length * (np.arange(SLABS)[:, None] * np.arange(INNER)[None, :])
    return np.stack([np.cos(angles), -np.sin(angles)]).astype(np.float32)


def rotate(value, turn, length, sign):
    re, im = value
    if turn == 0:
        return value
    if 4 * turn == length:
        return (-im, re) if sign > 0 else (im, -re)
    half = math.sqrt(0.5)
    if 8 * turn == length:
        return ((re - im) * half, (re + im) * half) if sign > 0 else ((re + im) * half, (im - re) * half)
    if 8 * turn == 3 * length:
        return ((-re - im) * half, (re - im) * half) if sign > 0 else ((im - re) * half, (-re - im) * half)
    cosine = math.cos(2.0 * math.pi * turn / length)
    sine = sign * math.sin(2.0 * math.pi * turn / length)
    return re * cosine - im * sine, re * sine + im * cosine


def butterflies(values, sign):
    length = len(values)
    if length == 1:
        return values
    even = butterflies(values[0::2], sign)
    odd = butterflies(values[1::2], sign)
    lower, upper = [], []
    for turn in range(length // 2):
        er, ei = even[turn]
        tr, ti = rotate(odd[turn], turn, length, sign)
        lower.append((er + tr, ei + ti))
        upper.append((er - tr, ei - ti))
    return lower + upper


def times(re, im, cr, ci):
    return re * cr - im * ci, re * ci + im * cr


def compress(x_ref, fwd_ref, inv_ref, tw_ref, chirp_ref, mid_ref, y_ref):
    def first(tile, carry):
        rows = pl.ds(pl.multiple_of(tile * 8, 8), 8)
        values = [
            (x_ref[0, 0, rows, a * INNER : (a + 1) * INNER], x_ref[0, 1, rows, a * INNER : (a + 1) * INNER])
            for a in range(SLABS)
        ]
        for k, (re, im) in enumerate(butterflies(values, -1)):
            re, im = times(re, im, tw_ref[0, k : k + 1, :], tw_ref[1, k : k + 1, :])
            mid_ref[k, rows, :INNER] = re
            mid_ref[k, rows, INNER:] = im
        return carry

    lax.fori_loop(0, ROWS // 8, first, 0)

    group = 256 // ROWS
    chains = 2

    def middle(step, carry):
        spans = [pl.ds(pl.multiple_of((step * chains + c) * group, group), group) for c in range(chains)]
        spectra = [dot3(split(mid_ref[ks].reshape(256, 2 * INNER)), (fwd_ref[0], fwd_ref[1])) for ks in spans]
        for ks, spec in zip(spans, spectra):
            spec = spec.reshape(group, ROWS, 2 * INNER)
            cr = chirp_ref[0, ks, :].reshape(group, 1, INNER)
            ci = chirp_ref[1, ks, :].reshape(group, 1, INNER)
            re, im = times(spec[:, :, :INNER], spec[:, :, INNER:], cr, ci)
            filtered = jnp.concatenate([re, im], axis=2).reshape(256, 2 * INNER)
            back = dot3(split(filtered), (inv_ref[0], inv_ref[1])).reshape(group, ROWS, 2 * INNER)
            tr = tw_ref[0, ks, :].reshape(group, 1, INNER)
            ti = tw_ref[1, ks, :].reshape(group, 1, INNER)
            re, im = times(back[:, :, :INNER], back[:, :, INNER:], tr, -ti)
            mid_ref[ks, :, :INNER] = re
            mid_ref[ks, :, INNER:] = im
        return carry

    lax.fori_loop(0, SLABS // (group * chains), middle, 0)

    def last(tile, carry):
        rows = pl.ds(pl.multiple_of(tile * 8, 8), 8)
        lower = pl.ds(pl.multiple_of(ROWS + tile * 8, 8), 8)
        values = [(mid_ref[k, rows, :INNER], mid_ref[k, rows, INNER:]) for k in range(SLABS)]
        for a, (re, im) in enumerate(butterflies(values, 1)):
            y_ref[a, rows, :] = re
            y_ref[a, lower, :] = im
        return carry

    lax.fori_loop(0, ROWS // 8, last, 0)
    y_ref[SLABS] = jnp.zeros((2 * ROWS, INNER), jnp.float32)


def windows(offset_ref, y_ref, z0_ref, z1_ref):
    lanes = lax.broadcasted_iota(jnp.int32, (2 * ROWS, INNER), 1)

    def window(step, carry):
        for part in range(4):
            dest = step * 4 + part
            for block in range(2):
                slab = 2 * dest + block
                back = INNER - offset_ref[slab]
                here = pltpu.roll(y_ref[slab], back, 1)
                after = pltpu.roll(y_ref[slab + 1], back, 1)
                shifted = jnp.where(lanes < back, here, after).reshape(2, ROWS, INNER)
                if block:
                    z1_ref[dest, 0] = shifted
                else:
                    z0_ref[dest] = shifted
        return carry

    lax.fori_loop(0, SLABS // 8, window, 0)


def early_kernel(x_ref, fwd_ref, inv_ref, tw_ref, chirp_ref, y_ref, mid_ref):
    compress(x_ref, fwd_ref, inv_ref, tw_ref, chirp_ref, mid_ref, y_ref.at[0])


def window_kernel(offset_ref, y_ref, z0_ref, z1_ref):
    windows(offset_ref, y_ref.at[0], z0_ref, z1_ref)


def late_kernel(offset_ref, x_ref, fwd_ref, inv_ref, tw_ref, chirp_ref, other_ref, z0_ref, z1_ref, mid_ref, y_ref):
    compress(x_ref, fwd_ref, inv_ref, tw_ref, chirp_ref, mid_ref, y_ref)
    windows(offset_ref, y_ref, z0_ref, z1_ref)


def table_specs():
    whole = pl.BlockSpec((2, 2 * INNER, 2 * INNER), lambda i, *_: (0, 0, 0))
    table = pl.BlockSpec((2, SLABS, INNER), lambda i, *_: (0, 0, 0))
    return [whole, whole, table, table]


def range_early(steps, echoes, tables):
    gates = echoes.shape[3]
    slabs = (SLABS + 1, 2 * ROWS, INNER)
    return pl.pallas_call(
        early_kernel,
        grid=(steps,),
        in_specs=[pl.BlockSpec((1, 2, ROWS, gates), lambda i: (0, 0, i, 0))] + table_specs(),
        out_specs=pl.BlockSpec((1, *slabs), lambda i: (i, 0, 0, 0)),
        out_shape=jax.ShapeDtypeStruct((steps, *slabs), jnp.float32),
        scratch_shapes=[pltpu.VMEM((SLABS, ROWS, 2 * INNER), jnp.float32)],
        name="range_early",
    )(echoes, *tables)


def block_shapes(dests, rows):
    return [
        jax.ShapeDtypeStruct((dests, 2, rows, BLOCK), jnp.float32),
        jax.ShapeDtypeStruct((dests, 2, 2, INNER, BLOCK), jnp.float32),
    ]


def block_specs(dests, start):
    tiles = INNER // ROWS
    return [
        pl.BlockSpec((dests, 2, ROWS, BLOCK), lambda i, *_: (0, 0, i, 0)),
        pl.BlockSpec((dests, 1, 2, ROWS, BLOCK), lambda i, *_: (0, (start + i) // tiles, 0, (start + i) % tiles, 0)),
    ]


def range_window(offsets, early):
    steps, slabs, _, _ = early.shape
    dests = slabs // 2
    return pl.pallas_call(
        window_kernel,
        grid_spec=pltpu.PrefetchScalarGridSpec(
            num_scalar_prefetch=1,
            grid=(steps,),
            in_specs=[pl.BlockSpec((1, slabs, 2 * ROWS, INNER), lambda i, *_: (i, 0, 0, 0))],
            out_specs=block_specs(dests, 0),
        ),
        out_shape=block_shapes(dests, steps * ROWS),
        name="range_window",
    )(offsets, early)


def range_late(start, offsets, echoes, tables, other):
    pulses, gates = echoes.shape[2], echoes.shape[3]
    dests = gates // (2 * BLOCK)
    steps = pulses // ROWS - start
    return pl.pallas_call(
        late_kernel,
        grid_spec=pltpu.PrefetchScalarGridSpec(
            num_scalar_prefetch=1,
            grid=(steps,),
            in_specs=[pl.BlockSpec((1, 2, ROWS, gates), lambda i, *_: (0, 0, start + i, 0))]
            + table_specs()
            + [pl.BlockSpec(memory_space=pl.ANY)],
            out_specs=block_specs(dests, start),
            scratch_shapes=[
                pltpu.VMEM((SLABS, ROWS, 2 * INNER), jnp.float32),
                pltpu.VMEM((SLABS + 1, 2 * ROWS, INNER), jnp.float32),
            ],
        ),
        out_shape=block_shapes(dests, steps * ROWS),
        input_output_aliases={6: 1},
        name="range_late",
    )(offsets, echoes, *tables, other)


def azimuth_kernel(count, place_ref, *refs):
    x_refs = refs[:count]
    fwd_ref, inv_ref, tw_ref, gain_ref = refs[count : count + 4]
    out_refs = refs[count + 4 : -4]
    mid_ref, wide_ref, o_ref, sem = refs[-4:]

    def slab(a, part, tile, upper):
        start = pl.multiple_of(tile * 8, 8)
        if count == 1:
            return x_refs[0][a // 2, a % 2, part, pl.ds(start, 8), :]
        rows = x_refs[0].shape[2]
        if a % 2 == 0 and not upper:
            return x_refs[0][a // 2, part, pl.ds(start, 8), :]
        return x_refs[1][a // 2, part, pl.ds(pl.multiple_of(start + (a % 2) * INNER - rows, 8), 8), :]

    def first(upper, tile, carry):
        start = pl.multiple_of(tile * 8, 8)
        rows = pl.ds(start, 8)
        lower = pl.ds(pl.multiple_of(INNER + tile * 8, 8), 8)
        values = [(slab(a, 0, tile, upper), slab(a, 1, tile, upper)) for a in range(SLABS)]
        tr, ti = tw_ref[0, rows, :], tw_ref[1, rows, :]
        gr, gi = gain_ref[0, rows, :], gain_ref[1, rows, :]
        for k, (re, im) in enumerate(butterflies(values, -1)):
            re, im = times(re, im, tr[:, k : k + 1], ti[:, k : k + 1])
            lane = slice((k % 2) * INNER, (k % 2 + 1) * INNER)
            mid_ref[k // 2, rows, lane] = re
            mid_ref[k // 2, lower, lane] = im
            wide_ref[k // 2, rows, lane] = jnp.broadcast_to(gr[:, k : k + 1], (8, INNER))
            wide_ref[k // 2, lower, lane] = jnp.broadcast_to(gi[:, k : k + 1], (8, INNER))
        return carry

    tiles = INNER // 8
    edge = x_refs[0].shape[2] // 8 if count == 2 else tiles
    lax.fori_loop(0, edge, functools.partial(first, False), 0)
    if edge < tiles:
        lax.fori_loop(edge, tiles, functools.partial(first, True), 0)

    def middle(step, carry):
        pairs = [2 * step, 2 * step + 1]
        spectra = [dot3((inv_ref[0], inv_ref[1]), split(mid_ref[pair])) for pair in pairs]
        for pair, spec in zip(pairs, spectra):
            re, im = times(spec[:INNER], spec[INNER:], wide_ref[pair, :INNER, :], wide_ref[pair, INNER:, :])
            mid_ref[pair] = dot3((fwd_ref[0], fwd_ref[1]), split(jnp.concatenate([re, im], axis=0)))
        return carry

    lax.fori_loop(0, SLABS // 4, middle, 0)

    def last(tile, carry):
        rows = pl.ds(pl.multiple_of(tile * 8, 8), 8)
        lower = pl.ds(pl.multiple_of(INNER + tile * 8, 8), 8)
        halves = (rows, lower)
        tr, ti = tw_ref[0, rows, :], tw_ref[1, rows, :]
        values = []
        for k in range(SLABS):
            lane = slice((k % 2) * INNER, (k % 2 + 1) * INNER)
            re, im = mid_ref[k // 2, rows, lane], mid_ref[k // 2, lower, lane]
            values.append(times(re, im, tr[:, k : k + 1], -ti[:, k : k + 1]))
        for a, (re, im) in enumerate(butterflies(values, 1)):
            o_ref[a // 2, 0, halves[a % 2], :] = re
            o_ref[a // 2, 1, halves[a % 2], :] = im
        return carry

    lax.fori_loop(0, INNER // 8, last, 0)

    place = place_ref[0]
    blocks = o_ref.shape[0]
    copies = []
    for block in range(blocks):
        source = o_ref.at[jnp.bitwise_xor(place, block)]
        if len(out_refs) == blocks:
            target = out_refs[block]
        else:
            source = o_ref.at[jnp.bitwise_xor(jnp.bitwise_and(place, 1), block)]
            target = out_refs[block % 2].at[block // 2]
        copies.append(pltpu.make_async_copy(source, target, sem.at[block]))
    for copy in copies:
        copy.start()
    for copy in copies:
        copy.wait()


def azimuth_filter(outs, place, received, fwd, inv, gain):
    vmem = pl.BlockSpec(memory_space=pltpu.VMEM)
    count = len(received)
    devices = received[0].shape[0]
    shape = (2, 2 * INNER, BLOCK)
    each = shape if outs == devices else (devices // outs, *shape)
    return pl.pallas_call(
        functools.partial(azimuth_kernel, count),
        in_specs=[pl.BlockSpec(memory_space=pltpu.SMEM)] + [vmem] * (count + 4),
        out_specs=[pl.BlockSpec(memory_space=pl.ANY)] * outs,
        out_shape=[jax.ShapeDtypeStruct(each, jnp.float32)] * outs,
        scratch_shapes=[
            pltpu.VMEM((SLABS // 2, 2 * INNER, 2 * INNER), jnp.float32),
            pltpu.VMEM((SLABS // 2, 2 * INNER, 2 * INNER), jnp.float32),
            pltpu.VMEM((devices, *shape), jnp.float32),
            pltpu.SemaphoreType.DMA((devices,)),
        ],
        name="azimuth_filter",
    )(place, *received, fwd, inv, jnp.asarray(twiddles().transpose(0, 2, 1)), gain)


def migrate_kernel(count, *refs):
    total = refs[0][...]
    if count == 1:
        total = jnp.sum(total, axis=0)
    for ref in refs[1:count]:
        total = total + ref[...]
    moved = jnp.dot(
        total.reshape(-1, BLOCK), refs[count][0], precision=lax.Precision.HIGHEST, preferred_element_type=jnp.float32
    )
    refs[-1][...] = moved.reshape(2, -1, BLOCK)


def migrate(block, parts, kernel, other=None):
    pulses = parts[0].shape[-2]
    args = [*parts, kernel]
    in_specs = [pl.BlockSpec(part.shape, lambda i, n=part.ndim: (0,) * n) for part in parts]
    in_specs.append(pl.BlockSpec((1, BLOCK, BLOCK), lambda i: (block, 0, 0)))
    aliases = {}
    if other is not None:
        in_specs.append(pl.BlockSpec(memory_space=pl.ANY))
        aliases = {len(args): 0}
        args.append(other)
    return pl.pallas_call(
        functools.partial(migrate_kernel, len(parts)),
        grid=(1,),
        in_specs=in_specs,
        out_specs=pl.BlockSpec((2, pulses, BLOCK), lambda i: (0, 0, block)),
        out_shape=jax.ShapeDtypeStruct((2, pulses, 2 * BLOCK), jnp.float32),
        input_output_aliases=aliases,
        name="migrate",
    )(*args)


def turn(blocks, axis, groups=None):
    return lax.all_to_all(blocks, axis, split_axis=0, concat_axis=0, tiled=True, axis_index_groups=groups)


def swap(block, distance):
    devices = range(lax.axis_size("chan"))
    return lax.ppermute(block, "chan", [(i, i ^ distance) for i in devices])


def body(echoes, chirp_phase, rcmc_kernel, rcmc_offset, az_phase, weight_table, weight_index):
    exact = lax.Precision.HIGHEST
    gates = echoes.shape[3]
    pulses = az_phase.shape[0]
    fwd_np, inv_np = inner_tables()
    fwd, inv = jnp.asarray(fwd_np), jnp.asarray(inv_np)
    devices = lax.axis_size("pulse")
    offsets = turn(jnp.broadcast_to(rcmc_offset, (devices, rcmc_offset.shape[0])), "pulse").reshape(-1)
    by_slab = chirp_phase.reshape(INNER, SLABS).T
    chirp = jnp.stack([jnp.cos(by_slab), jnp.sin(by_slab)]) * (1.0 / gates)
    tables = (fwd, inv, jnp.asarray(twiddles()), chirp)
    compressed = range_early(EARLY, echoes, tables)
    early, partial = range_window(offsets, compressed)
    late, full = range_late(EARLY, offsets, echoes, tables, partial)

    table_count = weight_table.shape[1]
    entry_ids = lax.broadcasted_iota(jnp.int32, (weight_index.shape[1], table_count), 1)
    one_hot = (weight_index[0][:, None] == entry_ids).astype(jnp.float32)
    chosen = jnp.dot(weight_table, one_hot.T, precision=exact) * (1.0 / pulses)
    weights = jnp.repeat(chosen, DBLOCK, axis=1)
    phases = az_phase.T
    gain = jnp.stack(times(jnp.cos(phases), jnp.sin(phases), weights[0:1], weights[1:2]))
    gain = gain.reshape(2, 2, INNER, SLABS)

    early = turn(early, "pulse")
    late = turn(late, "pulse")
    full = turn(full, "pulse")
    place = lax.axis_index("chan").astype(jnp.int32).reshape(1)
    channels = lax.axis_size("chan")
    first = azimuth_filter(channels, place, [early, late], fwd, inv, gain[:, 0])
    first = [first[0]] + [swap(first[k], k) for k in range(1, channels)]
    image = migrate(0, first, rcmc_kernel)
    keep, give = azimuth_filter(2, place, [full], fwd, inv, gain[:, 1])
    pair = keep + swap(give, 1)
    groups = [list(range(core, channels, 2)) for core in range(2)]
    second = turn(pair, "chan", groups)
    return migrate(1, [second], rcmc_kernel, image)


def solution(mesh):
    return jax.shard_map(
        body,
        mesh=mesh,
        in_specs=(
            P("chan", None, "pulse", None),
            P(),
            P("pulse", None, None),
            P("pulse"),
            P(None, "pulse"),
            P(),
            P("chan", None),
        ),
        out_specs=P(None, "chan", "pulse"),
        check_vma=False,
    )
```

```python
import functools
import math

import jax
import jax.numpy as jnp
import numpy as np
from jax import lax
from jax.experimental import pallas as pl
from jax.experimental.pallas import tpu as pltpu
from jax.sharding import PartitionSpec as P

BLOCK = 128
DBLOCK = 128
SLABS = 32
INNER = 128
ROWS = 32
EARLY = 1


def split(values):
    high = values.astype(jnp.bfloat16)
    low = (values - high.astype(jnp.float32)).astype(jnp.bfloat16)
    return high, low


def dot(left, right):
    return jnp.dot(left, right, preferred_element_type=jnp.float32)


def dot3(left, right):
    return dot(left[0], right[0]) + dot(left[0], right[1]) + dot(left[1], right[0])


def inner_tables():
    index = np.arange(INNER)
    angles = 2.0 * math.pi / INNER * (index[:, None] * index[None, :] % INNER)
    table = np.block([[np.cos(angles), -np.sin(angles)], [np.sin(angles), np.cos(angles)]])
    bf16 = jnp.bfloat16.dtype
    high = table.astype(np.float32).astype(bf16)
    low = (table - high.astype(np.float64)).astype(np.float32).astype(bf16)
    return np.stack([high, low]), np.stack([high.T, low.T])


def twiddles():
    length = SLABS * INNER
    angles = 2.0 * math.pi / length * (np.arange(SLABS)[:, None] * np.arange(INNER)[None, :])
    return np.stack([np.cos(angles), -np.sin(angles)]).astype(np.float32)


def rotate(value, turn, length, sign):
    re, im = value
    if turn == 0:
        return value
    if 4 * turn == length:
        return (-im, re) if sign > 0 else (im, -re)
    half = math.sqrt(0.5)
    if 8 * turn == length:
        return ((re - im) * half, (re + im) * half) if sign > 0 else ((re + im) * half, (im - re) * half)
    if 8 * turn == 3 * length:
        return ((-re - im) * half, (re - im) * half) if sign > 0 else ((im - re) * half, (-re - im) * half)
    cosine = math.cos(2.0 * math.pi * turn / length)
    sine = sign * math.sin(2.0 * math.pi * turn / length)
    return re * cosine - im * sine, re * sine + im * cosine


def butterflies(values, sign):
    length = len(values)
    if length == 1:
        return values
    even = butterflies(values[0::2], sign)
    odd = butterflies(values[1::2], sign)
    lower, upper = [], []
    for turn in range(length // 2):
        er, ei = even[turn]
        tr, ti = rotate(odd[turn], turn, length, sign)
        lower.append((er + tr, ei + ti))
        upper.append((er - tr, ei - ti))
    return lower + upper


def times(re, im, cr, ci):
    return re * cr - im * ci, re * ci + im * cr


def compress(x_ref, fwd_ref, inv_ref, tw_ref, chirp_ref, mid_ref, y_ref):
    def first(tile, carry):
        rows = pl.ds(pl.multiple_of(tile * 8, 8), 8)
        values = [
            (x_ref[0, 0, rows, a * INNER : (a + 1) * INNER], x_ref[0, 1, rows, a * INNER : (a + 1) * INNER])
            for a in range(SLABS)
        ]
        for k, (re, im) in enumerate(butterflies(values, -1)):
            re, im = times(re, im, tw_ref[0, k : k + 1, :], tw_ref[1, k : k + 1, :])
            mid_ref[k, rows, :INNER] = re
            mid_ref[k, rows, INNER:] = im
        return carry

    lax.fori_loop(0, ROWS // 8, first, 0)

    group = 256 // ROWS
    chains = 2

    def middle(step, carry):
        spans = [pl.ds(pl.multiple_of((step * chains + c) * group, group), group) for c in range(chains)]
        spectra = [dot3(split(mid_ref[ks].reshape(256, 2 * INNER)), (fwd_ref[0], fwd_ref[1])) for ks in spans]
        for ks, spec in zip(spans, spectra):
            spec = spec.reshape(group, ROWS, 2 * INNER)
            cr = chirp_ref[0, ks, :].reshape(group, 1, INNER)
            ci = chirp_ref[1, ks, :].reshape(group, 1, INNER)
            re, im = times(spec[:, :, :INNER], spec[:, :, INNER:], cr, ci)
            filtered = jnp.concatenate([re, im], axis=2).reshape(256, 2 * INNER)
            back = dot3(split(filtered), (inv_ref[0], inv_ref[1])).reshape(group, ROWS, 2 * INNER)
            tr = tw_ref[0, ks, :].reshape(group, 1, INNER)
            ti = tw_ref[1, ks, :].reshape(group, 1, INNER)
            re, im = times(back[:, :, :INNER], back[:, :, INNER:], tr, -ti)
            mid_ref[ks, :, :INNER] = re
            mid_ref[ks, :, INNER:] = im
        return carry

    lax.fori_loop(0, SLABS // (group * chains), middle, 0)

    def last(tile, carry):
        rows = pl.ds(pl.multiple_of(tile * 8, 8), 8)
        lower = pl.ds(pl.multiple_of(ROWS + tile * 8, 8), 8)
        values = [(mid_ref[k, rows, :INNER], mid_ref[k, rows, INNER:]) for k in range(SLABS)]
        for a, (re, im) in enumerate(butterflies(values, 1)):
            y_ref[a, rows, :] = re
            y_ref[a, lower, :] = im
        return carry

    lax.fori_loop(0, ROWS // 8, last, 0)
    y_ref[SLABS] = jnp.zeros((2 * ROWS, INNER), jnp.float32)


def windows(offset_ref, y_ref, z0_ref, za_ref, zb_ref):
    lanes = lax.broadcasted_iota(jnp.int32, (2 * ROWS, INNER), 1)
    upper = pl.program_id(0) % 2
    mine = lanes // (INNER // 2) == upper

    def window(step, carry):
        for part in range(2):
            dest = step * 2 + part
            for block in range(2):
                slab = 2 * dest + block
                back = INNER - offset_ref[slab]
                here = pltpu.roll(y_ref[slab], back, 1)
                after = pltpu.roll(y_ref[slab + 1], back, 1)
                gates = jnp.where(lanes < back, here, after)
                if block == 0:
                    z0_ref[dest, 0] = gates.reshape(2, ROWS, INNER)
                else:
                    other = pltpu.roll(gates, INNER // 2, 1)
                    for z_ref, value in (
                        (za_ref, jnp.where(upper == 0, gates, other)),
                        (zb_ref, jnp.where(upper == 0, other, gates)),
                    ):
                        held = z_ref[dest].reshape(2 * ROWS, INNER)
                        z_ref[dest] = jnp.where(mine, value, held).reshape(2, ROWS, INNER)
        return carry

    lax.fori_loop(0, SLABS // 4, window, 0)


def early_kernel(x_ref, fwd_ref, inv_ref, tw_ref, chirp_ref, y_ref, mid_ref):
    compress(x_ref, fwd_ref, inv_ref, tw_ref, chirp_ref, mid_ref, y_ref.at[0])


def window_kernel(offset_ref, y_ref, z0_ref, za_ref, zb_ref):
    windows(offset_ref, y_ref.at[0], z0_ref, za_ref, zb_ref)


def late_kernel(offset_ref, x_ref, fwd_ref, inv_ref, tw_ref, chirp_ref, *refs):
    z0_ref, za_ref, zb_ref, mid_ref, y_ref = refs[2:]
    compress(x_ref, fwd_ref, inv_ref, tw_ref, chirp_ref, mid_ref, y_ref)
    windows(offset_ref, y_ref, z0_ref, za_ref, zb_ref)


def table_specs():
    whole = pl.BlockSpec((2, 2 * INNER, 2 * INNER), lambda i, *_: (0, 0, 0))
    table = pl.BlockSpec((2, SLABS, INNER), lambda i, *_: (0, 0, 0))
    return [whole, whole, table, table]


def echo_spec(start, gates):
    return pl.BlockSpec((1, 2, ROWS, gates), lambda i, *_: (0, 0, (i % 2) * (INNER // ROWS) + start + i // 2, 0))


def range_early(tiles, echoes, tables):
    slabs = (SLABS + 1, 2 * ROWS, INNER)
    return pl.pallas_call(
        early_kernel,
        grid=(2 * tiles,),
        in_specs=[echo_spec(0, echoes.shape[3])] + table_specs(),
        out_specs=pl.BlockSpec((1, *slabs), lambda i: (i, 0, 0, 0)),
        out_shape=jax.ShapeDtypeStruct((2 * tiles, *slabs), jnp.float32),
        scratch_shapes=[pltpu.VMEM((SLABS, ROWS, 2 * INNER), jnp.float32)],
        name="range_early",
    )(echoes, *tables)


def block_shapes(dests, rows):
    part = jax.ShapeDtypeStruct((dests, 2, INNER, BLOCK), jnp.float32)
    return [jax.ShapeDtypeStruct((dests, 2, 2, rows, BLOCK), jnp.float32), part, part]


def block_specs(dests, start):
    part = pl.BlockSpec((dests, 2, ROWS, BLOCK), lambda i, *_: (0, 0, start + i // 2, 0))
    return [pl.BlockSpec((dests, 1, 2, ROWS, BLOCK), lambda i, *_: (0, i % 2, 0, i // 2, 0)), part, part]


def range_window(offsets, early):
    steps, slabs, _, _ = early.shape
    dests = slabs // 2
    return pl.pallas_call(
        window_kernel,
        grid_spec=pltpu.PrefetchScalarGridSpec(
            num_scalar_prefetch=1,
            grid=(steps,),
            in_specs=[pl.BlockSpec((1, slabs, 2 * ROWS, INNER), lambda i, *_: (i, 0, 0, 0))],
            out_specs=block_specs(dests, 0),
        ),
        out_shape=block_shapes(dests, steps // 2 * ROWS),
        name="range_window",
    )(offsets, early)


def range_late(start, offsets, echoes, tables, parts):
    gates = echoes.shape[3]
    dests = gates // (2 * BLOCK)
    tiles = INNER // ROWS - start
    return pl.pallas_call(
        late_kernel,
        grid_spec=pltpu.PrefetchScalarGridSpec(
            num_scalar_prefetch=1,
            grid=(2 * tiles,),
            in_specs=[echo_spec(start, gates)] + table_specs() + [pl.BlockSpec(memory_space=pl.ANY)] * 2,
            out_specs=block_specs(dests, start),
            scratch_shapes=[
                pltpu.VMEM((SLABS, ROWS, 2 * INNER), jnp.float32),
                pltpu.VMEM((SLABS + 1, 2 * ROWS, INNER), jnp.float32),
            ],
        ),
        out_shape=block_shapes(dests, tiles * ROWS),
        input_output_aliases={6: 1, 7: 2},
        name="range_late",
    )(offsets, echoes, *tables, *parts)


def hand_out(place_ref, o_ref, keep_ref, give_ref, sem):
    core = jnp.bitwise_and(place_ref[0], 1)
    copies = []
    for block in range(o_ref.shape[0]):
        source = o_ref.at[jnp.bitwise_xor(core, block)]
        target = (keep_ref, give_ref)[block % 2].at[block // 2]
        copies.append(pltpu.make_async_copy(source, target, sem.at[block]))
    for copy in copies:
        copy.start()
    for copy in copies:
        copy.wait()


def azimuth_kernel(place_ref, early_ref, late_ref, fwd_ref, inv_ref, tw_ref, gain_ref, keep_ref, give_ref, mid_ref, wide_ref, o_ref, sem):
    edge = early_ref.shape[3] // 8

    def first(x_ref, base, tile, carry):
        start = pl.multiple_of(tile * 8, 8)
        rows = pl.ds(start, 8)
        lower = pl.ds(pl.multiple_of(INNER + tile * 8, 8), 8)
        here = pl.ds(pl.multiple_of((tile - base) * 8, 8), 8)
        values = [(x_ref[a // 2, a % 2, 0, here, :], x_ref[a // 2, a % 2, 1, here, :]) for a in range(SLABS)]
        tr, ti = tw_ref[0, rows, :], tw_ref[1, rows, :]
        gr, gi = gain_ref[0, rows, :], gain_ref[1, rows, :]
        for k, (re, im) in enumerate(butterflies(values, -1)):
            re, im = times(re, im, tr[:, k : k + 1], ti[:, k : k + 1])
            lane = slice((k % 2) * INNER, (k % 2 + 1) * INNER)
            mid_ref[k // 2, rows, lane] = re
            mid_ref[k // 2, lower, lane] = im
            wide_ref[k // 2, rows, lane] = jnp.broadcast_to(gr[:, k : k + 1], (8, INNER))
            wide_ref[k // 2, lower, lane] = jnp.broadcast_to(gi[:, k : k + 1], (8, INNER))
        return carry

    lax.fori_loop(0, edge, functools.partial(first, early_ref, 0), 0)
    lax.fori_loop(edge, INNER // 8, functools.partial(first, late_ref, edge), 0)

    def middle(step, carry):
        pairs = [2 * step, 2 * step + 1]
        spectra = [dot3((inv_ref[0], inv_ref[1]), split(mid_ref[pair])) for pair in pairs]
        for pair, spec in zip(pairs, spectra):
            re, im = times(spec[:INNER], spec[INNER:], wide_ref[pair, :INNER, :], wide_ref[pair, INNER:, :])
            mid_ref[pair] = dot3((fwd_ref[0], fwd_ref[1]), split(jnp.concatenate([re, im], axis=0)))
        return carry

    lax.fori_loop(0, SLABS // 4, middle, 0)

    def last(tile, carry):
        rows = pl.ds(pl.multiple_of(tile * 8, 8), 8)
        lower = pl.ds(pl.multiple_of(INNER + tile * 8, 8), 8)
        halves = (rows, lower)
        tr, ti = tw_ref[0, rows, :], tw_ref[1, rows, :]
        values = []
        for k in range(SLABS):
            lane = slice((k % 2) * INNER, (k % 2 + 1) * INNER)
            re, im = mid_ref[k // 2, rows, lane], mid_ref[k // 2, lower, lane]
            values.append(times(re, im, tr[:, k : k + 1], -ti[:, k : k + 1]))
        for a, (re, im) in enumerate(butterflies(values, 1)):
            o_ref[a // 2, 0, halves[a % 2], :] = re
            o_ref[a // 2, 1, halves[a % 2], :] = im
        return carry

    lax.fori_loop(0, INNER // 8, last, 0)

    hand_out(place_ref, o_ref, keep_ref, give_ref, sem)


def narrow_kernel(place_ref, x_ref, fwd_ref, inv_ref, tw_ref, gain_ref, keep_ref, give_ref, mid_ref, o_ref, sem):
    half = SLABS // 2
    high = lax.broadcasted_iota(jnp.int32, (8, INNER), 1) >= INNER // 2
    sign = jnp.where(high, -1.0, 1.0)

    def turned(re, im, k, direction):
        cosine = math.cos(2.0 * math.pi * k / SLABS)
        sine = direction * math.sin(2.0 * math.pi * k / SLABS)
        return times(re, im, jnp.where(high, cosine, 1.0), jnp.where(high, sine, 0.0))

    def crossed(value):
        return pltpu.roll(value, INNER // 2, 1) + sign * value

    def place_of(k):
        return k // 2, slice((k % 2) * INNER, (k % 2 + 1) * INNER)

    def first(tile, carry):
        rows = pl.ds(pl.multiple_of(tile * 8, 8), 8)
        lower = pl.ds(pl.multiple_of(INNER + tile * 8, 8), 8)
        values = [(x_ref[i, 0, rows, :], x_ref[i, 1, rows, :]) for i in range(half)]
        for k, (re, im) in enumerate(butterflies(values, -1)):
            pair, lane = place_of(k)
            re, im = turned(re, im, k, -1)
            re, im = times(crossed(re), crossed(im), tw_ref[pair, rows, lane], tw_ref[pair, lower, lane])
            mid_ref[pair, rows, lane] = re
            mid_ref[pair, lower, lane] = im
        return carry

    lax.fori_loop(0, INNER // 8, first, 0)

    def middle(step, carry):
        pairs = [2 * step, 2 * step + 1]
        spectra = [dot3((inv_ref[0], inv_ref[1]), split(mid_ref[pair])) for pair in pairs]
        for pair, spec in zip(pairs, spectra):
            re, im = times(spec[:INNER], spec[INNER:], gain_ref[pair, :INNER, :], gain_ref[pair, INNER:, :])
            mid_ref[pair] = dot3((fwd_ref[0], fwd_ref[1]), split(jnp.concatenate([re, im], axis=0)))
        return carry

    lax.fori_loop(0, half // 4, middle, 0)

    def last(tile, carry):
        rows = pl.ds(pl.multiple_of(tile * 8, 8), 8)
        lower = pl.ds(pl.multiple_of(INNER + tile * 8, 8), 8)
        values = []
        for k in range(half):
            pair, lane = place_of(k)
            re, im = times(
                mid_ref[pair, rows, lane], mid_ref[pair, lower, lane], tw_ref[pair, rows, lane], -tw_ref[pair, lower, lane]
            )
            values.append(turned(crossed(re), crossed(im), k, 1))
        for i, (re, im) in enumerate(butterflies(values, 1)):
            o_ref[i, 0, rows, :] = re
            o_ref[i, 1, rows, :] = im
        return carry

    lax.fori_loop(0, INNER // 8, last, 0)
    hand_out(place_ref, o_ref, keep_ref, give_ref, sem)


def widen_kernel(tw_ref, gain_ref, tw_wide_ref, gain_wide_ref):
    half = SLABS // 2
    high = lax.broadcasted_iota(jnp.int32, (8, INNER), 1) >= INNER // 2

    def spread(tile, carry):
        rows = pl.ds(pl.multiple_of(tile * 8, 8), 8)
        for source, target in ((tw_ref, tw_wide_ref), (gain_ref, gain_wide_ref)):
            for part in range(2):
                value = source[part, rows, :]
                where = pl.ds(pl.multiple_of(part * INNER + tile * 8, 8), 8)
                for k in range(half):
                    lane = slice((k % 2) * INNER, (k % 2 + 1) * INNER)
                    target[k // 2, where, lane] = jnp.where(high, value[:, k + half : k + half + 1], value[:, k : k + 1])
        return carry

    lax.fori_loop(0, INNER // 8, spread, 0)


def azimuth_twiddles():
    return jnp.asarray(twiddles().transpose(0, 2, 1))


def widen(gain):
    wide = jax.ShapeDtypeStruct((SLABS // 4, 2 * INNER, 2 * INNER), jnp.float32)
    return pl.pallas_call(widen_kernel, out_shape=[wide, wide], name="widen")(azimuth_twiddles(), gain)


def filter_call(kernel, place, operands, rows, pairs, extra):
    vmem = pl.BlockSpec(memory_space=pltpu.VMEM)
    devices = operands[0].shape[0]
    blocks = jax.ShapeDtypeStruct((devices // 2, 2, rows, BLOCK), jnp.float32)
    mid = pltpu.VMEM((pairs, 2 * INNER, 2 * INNER), jnp.float32)
    return pl.pallas_call(
        kernel,
        in_specs=[pl.BlockSpec(memory_space=pltpu.SMEM)] + [vmem] * len(operands),
        out_specs=[pl.BlockSpec(memory_space=pl.ANY)] * 2,
        out_shape=[blocks, blocks],
        scratch_shapes=[mid] * (1 + extra)
        + [pltpu.VMEM((devices, 2, rows, BLOCK), jnp.float32), pltpu.SemaphoreType.DMA((devices,))],
    )(place, *operands)


def azimuth_filter(place, early, late, fwd, inv, gain):
    operands = (early, late, fwd, inv, azimuth_twiddles(), gain)
    return filter_call(azimuth_kernel, place, operands, 2 * INNER, SLABS // 2, 1)


def narrow_filter(place, received, fwd, inv, wide):
    operands = (received, fwd, inv, *wide)
    return filter_call(narrow_kernel, place, operands, INNER, SLABS // 4, 0)


def pair_kernel(place_ref, keep_ref, other_ref, *out_refs):
    chip = place_ref[0] // 2
    for k, out_ref in enumerate(out_refs):
        block = jnp.bitwise_xor(chip, k)
        out_ref[...] = keep_ref[block] + other_ref[block]


def pair_add(place, keep, other):
    vmem = pl.BlockSpec(memory_space=pltpu.VMEM)
    chips, *block = keep.shape
    return pl.pallas_call(
        pair_kernel,
        in_specs=[pl.BlockSpec(memory_space=pltpu.SMEM), vmem, vmem],
        out_specs=[vmem] * chips,
        out_shape=[jax.ShapeDtypeStruct(tuple(block), jnp.float32)] * chips,
        name="pair_add",
    )(place, keep, other)


def settle_kernel(*refs):
    total = refs[0][...]
    for ref in refs[1:-1]:
        total = total + ref[...]
    refs[-1][...] = total


def settle(parts):
    return pl.pallas_call(
        settle_kernel, out_shape=jax.ShapeDtypeStruct(parts[0].shape, jnp.float32), name="settle"
    )(*parts)


def exact_dot(left, right):
    return jnp.dot(left, right, precision=lax.Precision.HIGHEST, preferred_element_type=jnp.float32)


def migrate_kernel(*refs):
    total = refs[0][...]
    for ref in refs[1:-2]:
        total = total + ref[...]
    refs[-1][...] = exact_dot(total.reshape(-1, BLOCK), refs[-2][0]).reshape(2, -1, BLOCK)


def migrate_last_kernel(a_ref, b_ref, kernel_ref, other_ref, o_ref):
    low = lax.broadcasted_iota(jnp.int32, (INNER, BLOCK), 1) < BLOCK // 2
    for part in range(2):
        first = a_ref[part]
        second = b_ref[0, part]
        for device in range(1, b_ref.shape[0]):
            second = second + b_ref[device, part]
        rows = (
            jnp.where(low, first, pltpu.roll(second, BLOCK // 2, 1)),
            jnp.where(low, pltpu.roll(first, BLOCK // 2, 1), second),
        )
        for half in range(2):
            o_ref[part, half * INNER : (half + 1) * INNER, :] = exact_dot(rows[half], kernel_ref[0])


def migrate(block, kernel_body, parts, kernel, pulses, other=None):
    args = [*parts, kernel]
    in_specs = [pl.BlockSpec(part.shape, lambda i, n=part.ndim: (0,) * n) for part in parts]
    in_specs.append(pl.BlockSpec((1, BLOCK, BLOCK), lambda i: (block, 0, 0)))
    aliases = {}
    if other is not None:
        in_specs.append(pl.BlockSpec(memory_space=pl.ANY))
        aliases = {len(args): 0}
        args.append(other)
    return pl.pallas_call(
        kernel_body,
        grid=(1,),
        in_specs=in_specs,
        out_specs=pl.BlockSpec((2, pulses, BLOCK), lambda i: (0, 0, block)),
        out_shape=jax.ShapeDtypeStruct((2, pulses, 2 * BLOCK), jnp.float32),
        input_output_aliases=aliases,
        name="migrate",
    )(*args)


def turn(blocks, axis, groups=None):
    return lax.all_to_all(blocks, axis, split_axis=0, concat_axis=0, tiled=True, axis_index_groups=groups)


def swap(block, distance):
    devices = range(lax.axis_size("chan"))
    return lax.ppermute(block, "chan", [(i, i ^ distance) for i in devices])


def body(echoes, chirp_phase, rcmc_kernel, rcmc_offset, az_phase, weight_table, weight_index):
    exact = lax.Precision.HIGHEST
    gates = echoes.shape[3]
    pulses = az_phase.shape[0]
    fwd_np, inv_np = inner_tables()
    fwd, inv = jnp.asarray(fwd_np), jnp.asarray(inv_np)
    devices = lax.axis_size("pulse")
    offsets = turn(jnp.broadcast_to(rcmc_offset, (devices, rcmc_offset.shape[0])), "pulse").reshape(-1)
    by_slab = chirp_phase.reshape(INNER, SLABS).T
    chirp = jnp.stack([jnp.cos(by_slab), jnp.sin(by_slab)]) * (1.0 / gates)
    tables = (fwd, inv, jnp.asarray(twiddles()), chirp)
    compressed = range_early(EARLY, echoes, tables)
    early, *parts = range_window(offsets, compressed)
    late, part_a, part_b = range_late(EARLY, offsets, echoes, tables, parts)

    table_count = weight_table.shape[1]
    entry_ids = lax.broadcasted_iota(jnp.int32, (weight_index.shape[1], table_count), 1)
    one_hot = (weight_index[0][:, None] == entry_ids).astype(jnp.float32)
    chosen = jnp.dot(weight_table, one_hot.T, precision=exact) * (1.0 / pulses)
    weights = jnp.repeat(chosen, DBLOCK, axis=1)
    phases = az_phase.T
    gain = jnp.stack(times(jnp.cos(phases), jnp.sin(phases), weights[0:1], weights[1:2]))
    gain = gain.reshape(2, 2, INNER, SLABS)

    early = turn(early, "pulse")
    late = turn(late, "pulse")
    part_a = turn(part_a, "pulse")
    part_b = turn(part_b, "pulse")
    place = lax.axis_index("chan").astype(jnp.int32).reshape(1)
    channels = lax.axis_size("chan")
    rows = pulses // channels
    wide = widen(gain[:, 1])
    keep, give = azimuth_filter(place, early, late, fwd, inv, gain[:, 0])
    first = pair_add(place, keep, swap(give, 1))
    first = [first[0]] + [swap(first[k], 2 * k) for k in range(1, channels // 2)]
    image = migrate(0, migrate_kernel, first, rcmc_kernel, rows)
    keep, give = narrow_filter(place, part_a, fwd, inv, wide)
    sum_a = pair_add(place, keep, swap(give, 1))
    sum_a = [sum_a[0]] + [swap(sum_a[k], 2 * k) for k in range(1, channels // 2)]
    sum_a = settle(sum_a)
    keep, give = narrow_filter(place, part_b, fwd, inv, wide)
    pair = keep + swap(give, 1)
    groups = [list(range(core, channels, 2)) for core in range(2)]
    sum_b = turn(pair, "chan", groups)
    return migrate(1, migrate_last_kernel, [sum_a, sum_b], rcmc_kernel, rows, image)


def solution(mesh):
    return jax.shard_map(
        body,
        mesh=mesh,
        in_specs=(
            P("chan", None, "pulse", None),
            P(),
            P("pulse", None, None),
            P("pulse"),
            P(None, "pulse"),
            P(),
            P("chan", None),
        ),
        out_specs=P(None, "chan", "pulse"),
        check_vma=False,
    )
```

```python
import functools
import math

import jax
import jax.numpy as jnp
import numpy as np
from jax import lax
from jax.experimental import pallas as pl
from jax.experimental.pallas import tpu as pltpu
from jax.sharding import PartitionSpec as P

BLOCK = 128
DBLOCK = 128
SLABS = 32
INNER = 128
ROWS = 32
EARLY = 1


def granted(mebibytes):
    return pltpu.CompilerParams(vmem_limit_bytes=mebibytes * 2**20)


def split(values):
    high = values.astype(jnp.bfloat16)
    low = (values - high.astype(jnp.float32)).astype(jnp.bfloat16)
    return high, low


def dot(left, right):
    return jnp.dot(left, right, preferred_element_type=jnp.float32)


def dot3(left, right):
    return dot(left[0], right[0]) + dot(left[0], right[1]) + dot(left[1], right[0])


def inner_tables():
    index = np.arange(INNER)
    angles = 2.0 * math.pi / INNER * (index[:, None] * index[None, :] % INNER)
    table = np.block([[np.cos(angles), -np.sin(angles)], [np.sin(angles), np.cos(angles)]])
    bf16 = jnp.bfloat16.dtype
    high = table.astype(np.float32).astype(bf16)
    low = (table - high.astype(np.float64)).astype(np.float32).astype(bf16)
    return np.stack([high, low]), np.stack([high.T, low.T])


def twiddles():
    length = SLABS * INNER
    angles = 2.0 * math.pi / length * (np.arange(SLABS)[:, None] * np.arange(INNER)[None, :])
    return np.stack([np.cos(angles), -np.sin(angles)]).astype(np.float32)


def rotate(value, turn, length, sign):
    re, im = value
    if turn == 0:
        return value
    if 4 * turn == length:
        return (-im, re) if sign > 0 else (im, -re)
    half = math.sqrt(0.5)
    if 8 * turn == length:
        return ((re - im) * half, (re + im) * half) if sign > 0 else ((re + im) * half, (im - re) * half)
    if 8 * turn == 3 * length:
        return ((-re - im) * half, (re - im) * half) if sign > 0 else ((im - re) * half, (-re - im) * half)
    cosine = math.cos(2.0 * math.pi * turn / length)
    sine = sign * math.sin(2.0 * math.pi * turn / length)
    return re * cosine - im * sine, re * sine + im * cosine


def butterflies(values, sign):
    length = len(values)
    if length == 1:
        return values
    even = butterflies(values[0::2], sign)
    odd = butterflies(values[1::2], sign)
    lower, upper = [], []
    for turn in range(length // 2):
        er, ei = even[turn]
        tr, ti = rotate(odd[turn], turn, length, sign)
        lower.append((er + tr, ei + ti))
        upper.append((er - tr, ei - ti))
    return lower + upper


def times(re, im, cr, ci):
    return re * cr - im * ci, re * ci + im * cr


def compress(x_ref, fwd_ref, inv_ref, tw_ref, chirp_ref, mid_ref, y_ref):
    def first(tile, carry):
        rows = pl.ds(pl.multiple_of(tile * 8, 8), 8)
        values = [
            (x_ref[0, 0, rows, a * INNER : (a + 1) * INNER], x_ref[0, 1, rows, a * INNER : (a + 1) * INNER])
            for a in range(SLABS)
        ]
        for k, (re, im) in enumerate(butterflies(values, -1)):
            re, im = times(re, im, tw_ref[0, k : k + 1, :], tw_ref[1, k : k + 1, :])
            mid_ref[k, rows, :INNER] = re
            mid_ref[k, rows, INNER:] = im
        return carry

    lax.fori_loop(0, ROWS // 8, first, 0)

    group = 256 // ROWS
    chains = 2

    def middle(step, carry):
        spans = [pl.ds(pl.multiple_of((step * chains + c) * group, group), group) for c in range(chains)]
        spectra = [dot3(split(mid_ref[ks].reshape(256, 2 * INNER)), (fwd_ref[0], fwd_ref[1])) for ks in spans]
        for ks, spec in zip(spans, spectra):
            spec = spec.reshape(group, ROWS, 2 * INNER)
            cr = chirp_ref[0, ks, :].reshape(group, 1, INNER)
            ci = chirp_ref[1, ks, :].reshape(group, 1, INNER)
            re, im = times(spec[:, :, :INNER], spec[:, :, INNER:], cr, ci)
            filtered = jnp.concatenate([re, im], axis=2).reshape(256, 2 * INNER)
            back = dot3(split(filtered), (inv_ref[0], inv_ref[1])).reshape(group, ROWS, 2 * INNER)
            tr = tw_ref[0, ks, :].reshape(group, 1, INNER)
            ti = tw_ref[1, ks, :].reshape(group, 1, INNER)
            re, im = times(back[:, :, :INNER], back[:, :, INNER:], tr, -ti)
            mid_ref[ks, :, :INNER] = re
            mid_ref[ks, :, INNER:] = im
        return carry

    lax.fori_loop(0, SLABS // (group * chains), middle, 0)

    def last(tile, carry):
        rows = pl.ds(pl.multiple_of(tile * 8, 8), 8)
        lower = pl.ds(pl.multiple_of(ROWS + tile * 8, 8), 8)
        values = [(mid_ref[k, rows, :INNER], mid_ref[k, rows, INNER:]) for k in range(SLABS)]
        for a, (re, im) in enumerate(butterflies(values, 1)):
            y_ref[a, rows, :] = re
            y_ref[a, lower, :] = im
        return carry

    lax.fori_loop(0, ROWS // 8, last, 0)
    y_ref[SLABS] = jnp.zeros((2 * ROWS, INNER), jnp.float32)


def windows(offset_ref, y_ref, z0_ref, za_ref, zb_ref):
    lanes = lax.broadcasted_iota(jnp.int32, (2 * ROWS, INNER), 1)
    upper = pl.program_id(0) % 2
    mine = lanes // (INNER // 2) == upper

    def window(step, carry):
        for part in range(2):
            dest = step * 2 + part
            for block in range(2):
                slab = 2 * dest + block
                back = INNER - offset_ref[dest, 0, block]
                here = pltpu.roll(y_ref[slab], back, 1)
                after = pltpu.roll(y_ref[slab + 1], back, 1)
                gates = jnp.where(lanes < back, here, after)
                if block == 0:
                    z0_ref[dest, 0] = gates.reshape(2, ROWS, INNER)
                else:
                    other = pltpu.roll(gates, INNER // 2, 1)
                    for z_ref, value in (
                        (za_ref, jnp.where(upper == 0, gates, other)),
                        (zb_ref, jnp.where(upper == 0, other, gates)),
                    ):
                        held = z_ref[dest].reshape(2 * ROWS, INNER)
                        z_ref[dest] = jnp.where(mine, value, held).reshape(2, ROWS, INNER)
        return carry

    lax.fori_loop(0, SLABS // 4, window, 0)


def early_kernel(x_ref, fwd_ref, inv_ref, tw_ref, chirp_ref, y_ref, mid_ref):
    compress(x_ref, fwd_ref, inv_ref, tw_ref, chirp_ref, mid_ref, y_ref.at[0])


def window_kernel(offset_ref, y_ref, z0_ref, za_ref, zb_ref):
    windows(offset_ref, y_ref.at[0], z0_ref, za_ref, zb_ref)


def late_kernel(offset_ref, x_ref, fwd_ref, inv_ref, tw_ref, chirp_ref, *refs):
    z0_ref, za_ref, zb_ref, mid_ref, y_ref = refs[2:]
    compress(x_ref, fwd_ref, inv_ref, tw_ref, chirp_ref, mid_ref, y_ref)
    windows(offset_ref, y_ref, z0_ref, za_ref, zb_ref)


def table_specs():
    whole = pl.BlockSpec((2, 2 * INNER, 2 * INNER), lambda i, *_: (0, 0, 0))
    table = pl.BlockSpec((2, SLABS, INNER), lambda i, *_: (0, 0, 0))
    return [whole, whole, table, table]


def echo_spec(start, gates):
    return pl.BlockSpec((1, 2, ROWS, gates), lambda i, *_: (0, 0, (i % 2) * (INNER // ROWS) + start + i // 2, 0))


def range_early(tiles, echoes, tables):
    slabs = (SLABS + 1, 2 * ROWS, INNER)
    return pl.pallas_call(
        early_kernel,
        grid=(2 * tiles,),
        in_specs=[echo_spec(0, echoes.shape[3])] + table_specs(),
        out_specs=pl.BlockSpec((1, *slabs), lambda i: (i, 0, 0, 0)),
        out_shape=jax.ShapeDtypeStruct((2 * tiles, *slabs), jnp.float32),
        scratch_shapes=[pltpu.VMEM((SLABS, ROWS, 2 * INNER), jnp.float32)],
        name="range_early",
    )(echoes, *tables)


def block_shapes(dests, rows):
    part = jax.ShapeDtypeStruct((dests, 2, INNER, BLOCK), jnp.float32)
    return [jax.ShapeDtypeStruct((dests, 2, 2, rows, BLOCK), jnp.float32), part, part]


def block_specs(dests, start):
    part = pl.BlockSpec((dests, 2, ROWS, BLOCK), lambda i, *_: (0, 0, start + i // 2, 0))
    return [pl.BlockSpec((dests, 1, 2, ROWS, BLOCK), lambda i, *_: (0, i % 2, 0, i // 2, 0)), part, part]


def range_window(offsets, early):
    steps, slabs, _, _ = early.shape
    dests = slabs // 2
    return pl.pallas_call(
        window_kernel,
        grid_spec=pltpu.PrefetchScalarGridSpec(
            num_scalar_prefetch=1,
            grid=(steps,),
            in_specs=[pl.BlockSpec((1, slabs, 2 * ROWS, INNER), lambda i, *_: (i, 0, 0, 0))],
            out_specs=block_specs(dests, 0),
        ),
        out_shape=block_shapes(dests, steps // 2 * ROWS),
        name="range_window",
    )(offsets, early)


def range_late(start, offsets, echoes, tables, parts):
    gates = echoes.shape[3]
    dests = gates // (2 * BLOCK)
    tiles = INNER // ROWS - start
    return pl.pallas_call(
        late_kernel,
        grid_spec=pltpu.PrefetchScalarGridSpec(
            num_scalar_prefetch=1,
            grid=(2 * tiles,),
            in_specs=[echo_spec(start, gates)] + table_specs() + [pl.BlockSpec(memory_space=pl.ANY)] * 2,
            out_specs=block_specs(dests, start),
            scratch_shapes=[
                pltpu.VMEM((SLABS, ROWS, 2 * INNER), jnp.float32),
                pltpu.VMEM((SLABS + 1, 2 * ROWS, INNER), jnp.float32),
            ],
        ),
        out_shape=block_shapes(dests, tiles * ROWS),
        input_output_aliases={6: 1, 7: 2},
        name="range_late",
    )(offsets, echoes, *tables, *parts)


def hand_out(place_ref, o_ref, keep_ref, give_ref, sem):
    core = jnp.bitwise_and(place_ref[0], 1)
    copies = []
    for block in range(o_ref.shape[0]):
        source = o_ref.at[jnp.bitwise_xor(core, block)]
        target = (keep_ref, give_ref)[block % 2].at[block // 2]
        copies.append(pltpu.make_async_copy(source, target, sem.at[block]))
    for copy in copies:
        copy.start()
    for copy in copies:
        copy.wait()


def azimuth_kernel(place_ref, early_ref, late_ref, fwd_ref, inv_ref, tw_ref, gain_ref, keep_ref, give_ref, mid_ref, wide_ref, o_ref, sem):
    edge = early_ref.shape[3] // 8

    def first(x_ref, base, tile, carry):
        start = pl.multiple_of(tile * 8, 8)
        rows = pl.ds(start, 8)
        lower = pl.ds(pl.multiple_of(INNER + tile * 8, 8), 8)
        here = pl.ds(pl.multiple_of((tile - base) * 8, 8), 8)
        values = [(x_ref[a // 2, a % 2, 0, here, :], x_ref[a // 2, a % 2, 1, here, :]) for a in range(SLABS)]
        tr, ti = tw_ref[0, rows, :], tw_ref[1, rows, :]
        gr, gi = gain_ref[0, rows, :], gain_ref[1, rows, :]
        for k, (re, im) in enumerate(butterflies(values, -1)):
            re, im = times(re, im, tr[:, k : k + 1], ti[:, k : k + 1])
            lane = slice((k % 2) * INNER, (k % 2 + 1) * INNER)
            mid_ref[k // 2, rows, lane] = re
            mid_ref[k // 2, lower, lane] = im
            wide_ref[k // 2, rows, lane] = jnp.broadcast_to(gr[:, k : k + 1], (8, INNER))
            wide_ref[k // 2, lower, lane] = jnp.broadcast_to(gi[:, k : k + 1], (8, INNER))
        return carry

    lax.fori_loop(0, edge, functools.partial(first, early_ref, 0), 0)
    lax.fori_loop(edge, INNER // 8, functools.partial(first, late_ref, edge), 0)

    def middle(step, carry):
        pairs = [2 * step, 2 * step + 1]
        spectra = [dot3((inv_ref[0], inv_ref[1]), split(mid_ref[pair])) for pair in pairs]
        for pair, spec in zip(pairs, spectra):
            re, im = times(spec[:INNER], spec[INNER:], wide_ref[pair, :INNER, :], wide_ref[pair, INNER:, :])
            mid_ref[pair] = dot3((fwd_ref[0], fwd_ref[1]), split(jnp.concatenate([re, im], axis=0)))
        return carry

    lax.fori_loop(0, SLABS // 4, middle, 0)

    def last(tile, carry):
        rows = pl.ds(pl.multiple_of(tile * 8, 8), 8)
        lower = pl.ds(pl.multiple_of(INNER + tile * 8, 8), 8)
        halves = (rows, lower)
        tr, ti = tw_ref[0, rows, :], tw_ref[1, rows, :]
        values = []
        for k in range(SLABS):
            lane = slice((k % 2) * INNER, (k % 2 + 1) * INNER)
            re, im = mid_ref[k // 2, rows, lane], mid_ref[k // 2, lower, lane]
            values.append(times(re, im, tr[:, k : k + 1], -ti[:, k : k + 1]))
        for a, (re, im) in enumerate(butterflies(values, 1)):
            o_ref[a // 2, 0, halves[a % 2], :] = re
            o_ref[a // 2, 1, halves[a % 2], :] = im
        return carry

    lax.fori_loop(0, INNER // 8, last, 0)

    hand_out(place_ref, o_ref, keep_ref, give_ref, sem)


def narrow_kernel(place_ref, x_ref, fwd_ref, inv_ref, tw_ref, gain_ref, keep_ref, give_ref, mid_ref, o_ref, sem):
    half = SLABS // 2
    high = lax.broadcasted_iota(jnp.int32, (8, INNER), 1) >= INNER // 2
    sign = jnp.where(high, -1.0, 1.0)

    def turned(re, im, k, direction):
        cosine = math.cos(2.0 * math.pi * k / SLABS)
        sine = direction * math.sin(2.0 * math.pi * k / SLABS)
        return times(re, im, jnp.where(high, cosine, 1.0), jnp.where(high, sine, 0.0))

    def crossed(value):
        return pltpu.roll(value, INNER // 2, 1) + sign * value

    def place_of(k):
        return k // 2, slice((k % 2) * INNER, (k % 2 + 1) * INNER)

    def first(tile, carry):
        rows = pl.ds(pl.multiple_of(tile * 8, 8), 8)
        lower = pl.ds(pl.multiple_of(INNER + tile * 8, 8), 8)
        values = [(x_ref[i, 0, rows, :], x_ref[i, 1, rows, :]) for i in range(half)]
        for k, (re, im) in enumerate(butterflies(values, -1)):
            pair, lane = place_of(k)
            re, im = turned(re, im, k, -1)
            re, im = times(crossed(re), crossed(im), tw_ref[pair, rows, lane], tw_ref[pair, lower, lane])
            mid_ref[pair, rows, lane] = re
            mid_ref[pair, lower, lane] = im
        return carry

    lax.fori_loop(0, INNER // 8, first, 0)

    def middle(step, carry):
        pairs = [2 * step, 2 * step + 1]
        spectra = [dot3((inv_ref[0], inv_ref[1]), split(mid_ref[pair])) for pair in pairs]
        for pair, spec in zip(pairs, spectra):
            re, im = times(spec[:INNER], spec[INNER:], gain_ref[pair, :INNER, :], gain_ref[pair, INNER:, :])
            mid_ref[pair] = dot3((fwd_ref[0], fwd_ref[1]), split(jnp.concatenate([re, im], axis=0)))
        return carry

    lax.fori_loop(0, half // 4, middle, 0)

    def last(tile, carry):
        rows = pl.ds(pl.multiple_of(tile * 8, 8), 8)
        lower = pl.ds(pl.multiple_of(INNER + tile * 8, 8), 8)
        values = []
        for k in range(half):
            pair, lane = place_of(k)
            re, im = times(
                mid_ref[pair, rows, lane], mid_ref[pair, lower, lane], tw_ref[pair, rows, lane], -tw_ref[pair, lower, lane]
            )
            values.append(turned(crossed(re), crossed(im), k, 1))
        for i, (re, im) in enumerate(butterflies(values, 1)):
            o_ref[i, 0, rows, :] = re
            o_ref[i, 1, rows, :] = im
        return carry

    lax.fori_loop(0, INNER // 8, last, 0)
    hand_out(place_ref, o_ref, keep_ref, give_ref, sem)


def widen_kernel(tw_ref, gain_ref, tw_wide_ref, gain_wide_ref):
    half = SLABS // 2
    high = lax.broadcasted_iota(jnp.int32, (8, INNER), 1) >= INNER // 2

    def spread(tile, carry):
        rows = pl.ds(pl.multiple_of(tile * 8, 8), 8)
        for source, target in ((tw_ref, tw_wide_ref), (gain_ref, gain_wide_ref)):
            for part in range(2):
                value = source[part, rows, :]
                where = pl.ds(pl.multiple_of(part * INNER + tile * 8, 8), 8)
                for k in range(half):
                    lane = slice((k % 2) * INNER, (k % 2 + 1) * INNER)
                    target[k // 2, where, lane] = jnp.where(high, value[:, k + half : k + half + 1], value[:, k : k + 1])
        return carry

    lax.fori_loop(0, INNER // 8, spread, 0)


def azimuth_twiddles():
    return jnp.asarray(twiddles().transpose(0, 2, 1))


def widen(gain):
    wide = jax.ShapeDtypeStruct((SLABS // 4, 2 * INNER, 2 * INNER), jnp.float32)
    return pl.pallas_call(widen_kernel, out_shape=[wide, wide], name="widen", compiler_params=granted(16))(azimuth_twiddles(), gain)


def filter_call(kernel, place, operands, rows, pairs, extra):
    vmem = pl.BlockSpec(memory_space=pltpu.VMEM)
    devices = operands[0].shape[0]
    blocks = jax.ShapeDtypeStruct((devices // 2, 2, rows, BLOCK), jnp.float32)
    mid = pltpu.VMEM((pairs, 2 * INNER, 2 * INNER), jnp.float32)
    return pl.pallas_call(
        kernel,
        in_specs=[pl.BlockSpec(memory_space=pltpu.SMEM)] + [vmem] * len(operands),
        out_specs=[pl.BlockSpec(memory_space=pl.ANY)] * 2,
        out_shape=[blocks, blocks],
        scratch_shapes=[mid] * (1 + extra)
        + [pltpu.VMEM((devices, 2, rows, BLOCK), jnp.float32), pltpu.SemaphoreType.DMA((devices,))],
        compiler_params=granted(20 + 8 * extra),
    )(place, *operands)


def azimuth_filter(place, early, late, fwd, inv, gain):
    operands = (early, late, fwd, inv, azimuth_twiddles(), gain)
    return filter_call(azimuth_kernel, place, operands, 2 * INNER, SLABS // 2, 1)


def narrow_filter(place, received, fwd, inv, wide):
    operands = (received, fwd, inv, *wide)
    return filter_call(narrow_kernel, place, operands, INNER, SLABS // 4, 0)


def pair_kernel(place_ref, keep_ref, other_ref, *out_refs):
    chip = place_ref[0] // 2
    for k, out_ref in enumerate(out_refs):
        block = jnp.bitwise_xor(chip, k)
        out_ref[...] = keep_ref[block] + other_ref[block]


def pair_add(place, keep, other):
    vmem = pl.BlockSpec(memory_space=pltpu.VMEM)
    chips, *block = keep.shape
    return pl.pallas_call(
        pair_kernel,
        in_specs=[pl.BlockSpec(memory_space=pltpu.SMEM), vmem, vmem],
        out_specs=[vmem] * chips,
        out_shape=[jax.ShapeDtypeStruct(tuple(block), jnp.float32)] * chips,
        name="pair_add",
        compiler_params=granted(16),
    )(place, keep, other)


def settle_kernel(*refs):
    total = refs[0][...]
    for ref in refs[1:-1]:
        total = total + ref[...]
    refs[-1][...] = total


def settle(parts):
    return pl.pallas_call(
        settle_kernel,
        out_shape=jax.ShapeDtypeStruct(parts[0].shape, jnp.float32),
        name="settle",
        compiler_params=granted(16),
    )(*parts)


def exact_dot(left, right):
    return jnp.dot(left, right, precision=lax.Precision.HIGHEST, preferred_element_type=jnp.float32)


def migrate_kernel(*refs):
    total = refs[0][...]
    for ref in refs[1:-2]:
        total = total + ref[...]
    refs[-1][...] = exact_dot(total.reshape(-1, BLOCK), refs[-2][0]).reshape(2, -1, BLOCK)


def migrate_last_kernel(a_ref, *refs):
    b_refs = refs[:-3]
    kernel_ref, o_ref = refs[-3], refs[-1]
    low = lax.broadcasted_iota(jnp.int32, (INNER, BLOCK), 1) < BLOCK // 2
    for part in range(2):
        first = a_ref[part]
        second = b_refs[0][part]
        for b_ref in b_refs[1:]:
            second = second + b_ref[part]
        rows = (
            jnp.where(low, first, pltpu.roll(second, BLOCK // 2, 1)),
            jnp.where(low, pltpu.roll(first, BLOCK // 2, 1), second),
        )
        for half in range(2):
            o_ref[part, half * INNER : (half + 1) * INNER, :] = exact_dot(rows[half], kernel_ref[0])


def migrate(block, kernel_body, parts, kernel, pulses, other=None):
    args = [*parts, kernel]
    in_specs = [pl.BlockSpec(part.shape, lambda i, n=part.ndim: (0,) * n) for part in parts]
    in_specs.append(pl.BlockSpec((1, BLOCK, BLOCK), lambda i: (block, 0, 0)))
    aliases = {}
    if other is not None:
        in_specs.append(pl.BlockSpec(memory_space=pl.ANY))
        aliases = {len(args): 0}
        args.append(other)
    return pl.pallas_call(
        kernel_body,
        grid=(1,),
        in_specs=in_specs,
        out_specs=pl.BlockSpec((2, pulses, BLOCK), lambda i: (0, 0, block)),
        out_shape=jax.ShapeDtypeStruct((2, pulses, 2 * BLOCK), jnp.float32),
        input_output_aliases=aliases,
        name="migrate",
        compiler_params=granted(16),
    )(*args)


def turn(blocks, axis):
    return lax.all_to_all(blocks, axis, split_axis=0, concat_axis=0, tiled=True)


def swap(block, distance):
    devices = range(lax.axis_size("chan"))
    return lax.ppermute(block, "chan", [(i, i ^ distance) for i in devices])


def body(echoes, chirp_phase, rcmc_kernel, rcmc_offset, az_phase, weight_table, weight_index):
    exact = lax.Precision.HIGHEST
    gates = echoes.shape[3]
    pulses = az_phase.shape[0]
    fwd_np, inv_np = inner_tables()
    fwd, inv = jnp.asarray(fwd_np), jnp.asarray(inv_np)
    devices = lax.axis_size("pulse")
    offsets = turn(jnp.broadcast_to(rcmc_offset, (devices, 1, rcmc_offset.shape[0])), "pulse")
    by_slab = chirp_phase.reshape(INNER, SLABS).T
    chirp = jnp.stack([jnp.cos(by_slab), jnp.sin(by_slab)]) * (1.0 / gates)
    tables = (fwd, inv, jnp.asarray(twiddles()), chirp)
    compressed = range_early(EARLY, echoes, tables)
    early, *parts = range_window(offsets, compressed)
    late, part_a, part_b = range_late(EARLY, offsets, echoes, tables, parts)

    table_count = weight_table.shape[1]
    entry_ids = lax.broadcasted_iota(jnp.int32, (weight_index.shape[1], table_count), 1)
    one_hot = (weight_index[0][:, None] == entry_ids).astype(jnp.float32)
    chosen = jnp.dot(weight_table, one_hot.T, precision=exact) * (1.0 / pulses)
    weights = jnp.repeat(chosen, DBLOCK, axis=1)
    phases = az_phase.T
    gain = jnp.stack(times(jnp.cos(phases), jnp.sin(phases), weights[0:1], weights[1:2]))
    gain = gain.reshape(2, 2, INNER, SLABS)

    early = turn(early, "pulse")
    late = turn(late, "pulse")
    part_a = turn(part_a, "pulse")
    part_b = turn(part_b, "pulse")
    place = lax.axis_index("chan").astype(jnp.int32).reshape(1)
    channels = lax.axis_size("chan")
    rows = pulses // channels
    wide = widen(gain[:, 1])
    keep, give = azimuth_filter(place, early, late, fwd, inv, gain[:, 0])
    first = pair_add(place, keep, swap(give, 1))
    first = [first[0]] + [swap(first[k], 2 * k) for k in range(1, channels // 2)]
    image = migrate(0, migrate_kernel, first, rcmc_kernel, rows)
    keep, give = narrow_filter(place, part_a, fwd, inv, wide)
    sum_a = pair_add(place, keep, swap(give, 1))
    sum_a = [sum_a[0]] + [swap(sum_a[k], 2 * k) for k in range(1, channels // 2)]
    sum_a = settle(sum_a)
    keep, give = narrow_filter(place, part_b, fwd, inv, wide)
    sum_b = pair_add(place, keep, swap(give, 1))
    sum_b = [sum_b[0]] + [swap(sum_b[k], 2 * k) for k in range(1, channels // 2)]
    return migrate(1, migrate_last_kernel, [sum_a, *sum_b], rcmc_kernel, rows, image)


def solution(mesh):
    return jax.shard_map(
        body,
        mesh=mesh,
        in_specs=(
            P("chan", None, "pulse", None),
            P(),
            P("pulse", None, None),
            P("pulse"),
            P(None, "pulse"),
            P(),
            P("chan", None),
        ),
        out_specs=P(None, "chan", "pulse"),
        check_vma=False,
    )
```

```python
import functools
import math

import jax
import jax.numpy as jnp
import numpy as np
from jax import lax
from jax.experimental import pallas as pl
from jax.experimental.pallas import tpu as pltpu
from jax.sharding import PartitionSpec as P

BLOCK = 128
DBLOCK = 128
SLABS = 32
INNER = 128
ROWS = 32
EARLY = 1


def granted(mebibytes):
    return pltpu.CompilerParams(vmem_limit_bytes=mebibytes * 2**20)


def split(values):
    high = values.astype(jnp.bfloat16)
    low = (values - high.astype(jnp.float32)).astype(jnp.bfloat16)
    return high, low


def dot(left, right):
    return jnp.dot(left, right, preferred_element_type=jnp.float32)


def dot3(left, right):
    return dot(left[0], right[0]) + dot(left[0], right[1]) + dot(left[1], right[0])


def inner_tables():
    index = np.arange(INNER)
    angles = 2.0 * math.pi / INNER * (index[:, None] * index[None, :] % INNER)
    table = np.block([[np.cos(angles), -np.sin(angles)], [np.sin(angles), np.cos(angles)]])
    bf16 = jnp.bfloat16.dtype
    high = table.astype(np.float32).astype(bf16)
    low = (table - high.astype(np.float64)).astype(np.float32).astype(bf16)
    return np.stack([high, low]), np.stack([high.T, low.T])


def twiddles():
    length = SLABS * INNER
    angles = 2.0 * math.pi / length * (np.arange(SLABS)[:, None] * np.arange(INNER)[None, :])
    return np.stack([np.cos(angles), -np.sin(angles)]).astype(np.float32)


def rotate(value, turn, length, sign):
    re, im = value
    if turn == 0:
        return value
    if 4 * turn == length:
        return (-im, re) if sign > 0 else (im, -re)
    half = math.sqrt(0.5)
    if 8 * turn == length:
        return ((re - im) * half, (re + im) * half) if sign > 0 else ((re + im) * half, (im - re) * half)
    if 8 * turn == 3 * length:
        return ((-re - im) * half, (re - im) * half) if sign > 0 else ((im - re) * half, (-re - im) * half)
    cosine = math.cos(2.0 * math.pi * turn / length)
    sine = sign * math.sin(2.0 * math.pi * turn / length)
    return re * cosine - im * sine, re * sine + im * cosine


def butterflies(values, sign):
    length = len(values)
    if length == 1:
        return values
    even = butterflies(values[0::2], sign)
    odd = butterflies(values[1::2], sign)
    lower, upper = [], []
    for turn in range(length // 2):
        er, ei = even[turn]
        tr, ti = rotate(odd[turn], turn, length, sign)
        lower.append((er + tr, ei + ti))
        upper.append((er - tr, ei - ti))
    return lower + upper


def times(re, im, cr, ci):
    return re * cr - im * ci, re * ci + im * cr


def compress(x_ref, fwd_ref, inv_ref, tw_ref, chirp_ref, mid_ref, y_ref):
    def first(tile, carry):
        rows = pl.ds(pl.multiple_of(tile * 8, 8), 8)
        values = [
            (x_ref[0, 0, rows, a * INNER : (a + 1) * INNER], x_ref[0, 1, rows, a * INNER : (a + 1) * INNER])
            for a in range(SLABS)
        ]
        for k, (re, im) in enumerate(butterflies(values, -1)):
            re, im = times(re, im, tw_ref[0, k : k + 1, :], tw_ref[1, k : k + 1, :])
            mid_ref[k, rows, :INNER] = re
            mid_ref[k, rows, INNER:] = im
        return carry

    lax.fori_loop(0, ROWS // 8, first, 0)

    group = 256 // ROWS
    chains = 2

    def middle(step, carry):
        spans = [pl.ds(pl.multiple_of((step * chains + c) * group, group), group) for c in range(chains)]
        spectra = [dot3(split(mid_ref[ks].reshape(256, 2 * INNER)), (fwd_ref[0], fwd_ref[1])) for ks in spans]
        for ks, spec in zip(spans, spectra):
            spec = spec.reshape(group, ROWS, 2 * INNER)
            cr = chirp_ref[0, ks, :].reshape(group, 1, INNER)
            ci = chirp_ref[1, ks, :].reshape(group, 1, INNER)
            re, im = times(spec[:, :, :INNER], spec[:, :, INNER:], cr, ci)
            filtered = jnp.concatenate([re, im], axis=2).reshape(256, 2 * INNER)
            back = dot3(split(filtered), (inv_ref[0], inv_ref[1])).reshape(group, ROWS, 2 * INNER)
            tr = tw_ref[0, ks, :].reshape(group, 1, INNER)
            ti = tw_ref[1, ks, :].reshape(group, 1, INNER)
            re, im = times(back[:, :, :INNER], back[:, :, INNER:], tr, -ti)
            mid_ref[ks, :, :INNER] = re
            mid_ref[ks, :, INNER:] = im
        return carry

    lax.fori_loop(0, SLABS // (group * chains), middle, 0)

    def last(tile, carry):
        rows = pl.ds(pl.multiple_of(tile * 8, 8), 8)
        lower = pl.ds(pl.multiple_of(ROWS + tile * 8, 8), 8)
        values = [(mid_ref[k, rows, :INNER], mid_ref[k, rows, INNER:]) for k in range(SLABS)]
        for a, (re, im) in enumerate(butterflies(values, 1)):
            y_ref[a, rows, :] = re
            y_ref[a, lower, :] = im
        return carry

    lax.fori_loop(0, ROWS // 8, last, 0)
    y_ref[SLABS] = jnp.zeros((2 * ROWS, INNER), jnp.float32)


def window_at(offset_ref, y_ref, dest, block, lanes):
    slab = 2 * dest + block
    back = INNER - offset_ref[dest, 0, block]
    here = pltpu.roll(y_ref[slab], back, 1)
    after = pltpu.roll(y_ref[slab + 1], back, 1)
    return jnp.where(lanes < back, here, after)


def first_windows(offset_ref, y_ref, z0_ref):
    lanes = lax.broadcasted_iota(jnp.int32, (2 * ROWS, INNER), 1)

    def window(step, carry):
        for part in range(4):
            dest = step * 4 + part
            z0_ref[dest, 0] = window_at(offset_ref, y_ref, dest, 0, lanes).reshape(2, ROWS, INNER)
        return carry

    lax.fori_loop(0, SLABS // 8, window, 0)


def second_windows(offset_ref, y_ref, za_ref, zb_ref):
    lanes = lax.broadcasted_iota(jnp.int32, (2 * ROWS, INNER), 1)
    upper = pl.program_id(0) % 2
    mine = lanes // (INNER // 2) == upper

    def window(step, carry):
        for part in range(2):
            dest = step * 2 + part
            gates = window_at(offset_ref, y_ref, dest, 1, lanes)
            other = pltpu.roll(gates, INNER // 2, 1)
            for z_ref, value in (
                (za_ref, jnp.where(upper == 0, gates, other)),
                (zb_ref, jnp.where(upper == 0, other, gates)),
            ):
                held = z_ref[dest].reshape(2 * ROWS, INNER)
                z_ref[dest] = jnp.where(mine, value, held).reshape(2, ROWS, INNER)
        return carry

    lax.fori_loop(0, SLABS // 4, window, 0)


def early_kernel(x_ref, fwd_ref, inv_ref, tw_ref, chirp_ref, y_ref, mid_ref):
    compress(x_ref, fwd_ref, inv_ref, tw_ref, chirp_ref, mid_ref, y_ref.at[0])


def first_kernel(offset_ref, y_ref, z0_ref):
    first_windows(offset_ref, y_ref.at[0], z0_ref)


def second_kernel(offset_ref, y_ref, za_ref, zb_ref):
    second_windows(offset_ref, y_ref.at[0], za_ref, zb_ref)


def late_kernel(offset_ref, x_ref, fwd_ref, inv_ref, tw_ref, chirp_ref, other_ref, z0_ref, y_ref, mid_ref):
    compress(x_ref, fwd_ref, inv_ref, tw_ref, chirp_ref, mid_ref, y_ref.at[0])
    first_windows(offset_ref, y_ref.at[0], z0_ref)


def table_specs():
    whole = pl.BlockSpec((2, 2 * INNER, 2 * INNER), lambda i, *_: (0, 0, 0))
    table = pl.BlockSpec((2, SLABS, INNER), lambda i, *_: (0, 0, 0))
    return [whole, whole, table, table]


def echo_spec(start, gates):
    return pl.BlockSpec((1, 2, ROWS, gates), lambda i, *_: (0, 0, (i % 2) * (INNER // ROWS) + start + i // 2, 0))


def compressed_shape(echoes):
    return jax.ShapeDtypeStruct((echoes.shape[2] // ROWS, SLABS + 1, 2 * ROWS, INNER), jnp.float32)


def compressed_spec(start):
    return pl.BlockSpec((1, SLABS + 1, 2 * ROWS, INNER), lambda i, *_: (2 * start + i, 0, 0, 0))


def range_early(tiles, echoes, tables):
    return pl.pallas_call(
        early_kernel,
        grid=(2 * tiles,),
        in_specs=[echo_spec(0, echoes.shape[3])] + table_specs(),
        out_specs=compressed_spec(0),
        out_shape=compressed_shape(echoes),
        scratch_shapes=[pltpu.VMEM((SLABS, ROWS, 2 * INNER), jnp.float32)],
        name="range_early",
    )(echoes, *tables)


def first_shape(tiles):
    return jax.ShapeDtypeStruct((SLABS // 2, 2, 2, tiles * ROWS, BLOCK), jnp.float32)


def first_spec():
    return pl.BlockSpec((SLABS // 2, 1, 2, ROWS, BLOCK), lambda i, *_: (0, i % 2, 0, i // 2, 0))


def window_first(tiles, offsets, compressed):
    return pl.pallas_call(
        first_kernel,
        grid_spec=pltpu.PrefetchScalarGridSpec(
            num_scalar_prefetch=1, grid=(2 * tiles,), in_specs=[compressed_spec(0)], out_specs=first_spec()
        ),
        out_shape=first_shape(tiles),
        name="window_first",
    )(offsets, compressed)


def range_late(start, offsets, echoes, tables, compressed):
    tiles = INNER // ROWS - start
    return pl.pallas_call(
        late_kernel,
        grid_spec=pltpu.PrefetchScalarGridSpec(
            num_scalar_prefetch=1,
            grid=(2 * tiles,),
            in_specs=[echo_spec(start, echoes.shape[3])] + table_specs() + [pl.BlockSpec(memory_space=pl.ANY)],
            out_specs=[first_spec(), compressed_spec(start)],
            scratch_shapes=[pltpu.VMEM((SLABS, ROWS, 2 * INNER), jnp.float32)],
        ),
        out_shape=[first_shape(tiles), compressed_shape(echoes)],
        input_output_aliases={6: 1},
        name="range_late",
    )(offsets, echoes, *tables, compressed)


def window_second(offsets, compressed):
    part = jax.ShapeDtypeStruct((SLABS // 2, 2, INNER, BLOCK), jnp.float32)
    spec = pl.BlockSpec((SLABS // 2, 2, ROWS, BLOCK), lambda i, *_: (0, 0, i // 2, 0))
    return pl.pallas_call(
        second_kernel,
        grid_spec=pltpu.PrefetchScalarGridSpec(
            num_scalar_prefetch=1, grid=(compressed.shape[0],), in_specs=[compressed_spec(0)], out_specs=[spec, spec]
        ),
        out_shape=[part, part],
        name="window_second",
    )(offsets, compressed)


def hand_out(place_ref, o_ref, keep_ref, give_ref, sem):
    core = jnp.bitwise_and(place_ref[0], 1)
    copies = []
    for block in range(o_ref.shape[0]):
        source = o_ref.at[jnp.bitwise_xor(core, block)]
        target = (keep_ref, give_ref)[block % 2].at[block // 2]
        copies.append(pltpu.make_async_copy(source, target, sem.at[block]))
    for copy in copies:
        copy.start()
    for copy in copies:
        copy.wait()


def azimuth_kernel(place_ref, early_ref, late_ref, fwd_ref, inv_ref, tw_ref, gain_ref, keep_ref, give_ref, mid_ref, wide_ref, o_ref, sem):
    edge = early_ref.shape[3] // 8

    def first(x_ref, base, tile, carry):
        start = pl.multiple_of(tile * 8, 8)
        rows = pl.ds(start, 8)
        lower = pl.ds(pl.multiple_of(INNER + tile * 8, 8), 8)
        here = pl.ds(pl.multiple_of((tile - base) * 8, 8), 8)
        values = [(x_ref[a // 2, a % 2, 0, here, :], x_ref[a // 2, a % 2, 1, here, :]) for a in range(SLABS)]
        tr, ti = tw_ref[0, rows, :], tw_ref[1, rows, :]
        gr, gi = gain_ref[0, rows, :], gain_ref[1, rows, :]
        for k, (re, im) in enumerate(butterflies(values, -1)):
            re, im = times(re, im, tr[:, k : k + 1], ti[:, k : k + 1])
            lane = slice((k % 2) * INNER, (k % 2 + 1) * INNER)
            mid_ref[k // 2, rows, lane] = re
            mid_ref[k // 2, lower, lane] = im
            wide_ref[k // 2, rows, lane] = jnp.broadcast_to(gr[:, k : k + 1], (8, INNER))
            wide_ref[k // 2, lower, lane] = jnp.broadcast_to(gi[:, k : k + 1], (8, INNER))
        return carry

    lax.fori_loop(0, edge, functools.partial(first, early_ref, 0), 0)
    lax.fori_loop(edge, INNER // 8, functools.partial(first, late_ref, edge), 0)

    def middle(step, carry):
        pairs = [2 * step, 2 * step + 1]
        spectra = [dot3((inv_ref[0], inv_ref[1]), split(mid_ref[pair])) for pair in pairs]
        for pair, spec in zip(pairs, spectra):
            re, im = times(spec[:INNER], spec[INNER:], wide_ref[pair, :INNER, :], wide_ref[pair, INNER:, :])
            mid_ref[pair] = dot3((fwd_ref[0], fwd_ref[1]), split(jnp.concatenate([re, im], axis=0)))
        return carry

    lax.fori_loop(0, SLABS // 4, middle, 0)

    def last(tile, carry):
        rows = pl.ds(pl.multiple_of(tile * 8, 8), 8)
        lower = pl.ds(pl.multiple_of(INNER + tile * 8, 8), 8)
        halves = (rows, lower)
        tr, ti = tw_ref[0, rows, :], tw_ref[1, rows, :]
        values = []
        for k in range(SLABS):
            lane = slice((k % 2) * INNER, (k % 2 + 1) * INNER)
            re, im = mid_ref[k // 2, rows, lane], mid_ref[k // 2, lower, lane]
            values.append(times(re, im, tr[:, k : k + 1], -ti[:, k : k + 1]))
        for a, (re, im) in enumerate(butterflies(values, 1)):
            o_ref[a // 2, 0, halves[a % 2], :] = re
            o_ref[a // 2, 1, halves[a % 2], :] = im
        return carry

    lax.fori_loop(0, INNER // 8, last, 0)

    hand_out(place_ref, o_ref, keep_ref, give_ref, sem)


def narrow_kernel(place_ref, x_ref, fwd_ref, inv_ref, tw_ref, gain_ref, keep_ref, give_ref, mid_ref, o_ref, sem):
    half = SLABS // 2
    high = lax.broadcasted_iota(jnp.int32, (8, INNER), 1) >= INNER // 2
    sign = jnp.where(high, -1.0, 1.0)

    def turned(re, im, k, direction):
        cosine = math.cos(2.0 * math.pi * k / SLABS)
        sine = direction * math.sin(2.0 * math.pi * k / SLABS)
        return times(re, im, jnp.where(high, cosine, 1.0), jnp.where(high, sine, 0.0))

    def crossed(value):
        return pltpu.roll(value, INNER // 2, 1) + sign * value

    def place_of(k):
        return k // 2, slice((k % 2) * INNER, (k % 2 + 1) * INNER)

    def first(tile, carry):
        rows = pl.ds(pl.multiple_of(tile * 8, 8), 8)
        lower = pl.ds(pl.multiple_of(INNER + tile * 8, 8), 8)
        values = [(x_ref[i, 0, rows, :], x_ref[i, 1, rows, :]) for i in range(half)]
        for k, (re, im) in enumerate(butterflies(values, -1)):
            pair, lane = place_of(k)
            re, im = turned(re, im, k, -1)
            re, im = times(crossed(re), crossed(im), tw_ref[pair, rows, lane], tw_ref[pair, lower, lane])
            mid_ref[pair, rows, lane] = re
            mid_ref[pair, lower, lane] = im
        return carry

    lax.fori_loop(0, INNER // 8, first, 0, unroll=2)

    def middle(step, carry):
        pairs = [2 * step, 2 * step + 1]
        spectra = [dot3((inv_ref[0], inv_ref[1]), split(mid_ref[pair])) for pair in pairs]
        for pair, spec in zip(pairs, spectra):
            re, im = times(spec[:INNER], spec[INNER:], gain_ref[pair, :INNER, :], gain_ref[pair, INNER:, :])
            mid_ref[pair] = dot3((fwd_ref[0], fwd_ref[1]), split(jnp.concatenate([re, im], axis=0)))
        return carry

    lax.fori_loop(0, half // 4, middle, 0)

    def last(tile, carry):
        rows = pl.ds(pl.multiple_of(tile * 8, 8), 8)
        lower = pl.ds(pl.multiple_of(INNER + tile * 8, 8), 8)
        values = []
        for k in range(half):
            pair, lane = place_of(k)
            re, im = times(
                mid_ref[pair, rows, lane], mid_ref[pair, lower, lane], tw_ref[pair, rows, lane], -tw_ref[pair, lower, lane]
            )
            values.append(turned(crossed(re), crossed(im), k, 1))
        for i, (re, im) in enumerate(butterflies(values, 1)):
            o_ref[i, 0, rows, :] = re
            o_ref[i, 1, rows, :] = im
        return carry

    lax.fori_loop(0, INNER // 8, last, 0, unroll=2)
    hand_out(place_ref, o_ref, keep_ref, give_ref, sem)


def widen_kernel(tw_ref, gain_ref, tw_wide_ref, gain_wide_ref):
    half = SLABS // 2
    high = lax.broadcasted_iota(jnp.int32, (8, INNER), 1) >= INNER // 2

    def spread(tile, carry):
        rows = pl.ds(pl.multiple_of(tile * 8, 8), 8)
        for source, target in ((tw_ref, tw_wide_ref), (gain_ref, gain_wide_ref)):
            for part in range(2):
                value = source[part, rows, :]
                where = pl.ds(pl.multiple_of(part * INNER + tile * 8, 8), 8)
                for k in range(half):
                    lane = slice((k % 2) * INNER, (k % 2 + 1) * INNER)
                    target[k // 2, where, lane] = jnp.where(high, value[:, k + half : k + half + 1], value[:, k : k + 1])
        return carry

    lax.fori_loop(0, INNER // 8, spread, 0)


def azimuth_twiddles():
    return jnp.asarray(twiddles().transpose(0, 2, 1))


def widen(gain):
    wide = jax.ShapeDtypeStruct((SLABS // 4, 2 * INNER, 2 * INNER), jnp.float32)
    return pl.pallas_call(widen_kernel, out_shape=[wide, wide], name="widen", compiler_params=granted(8))(azimuth_twiddles(), gain)


def filter_call(kernel, place, operands, rows, pairs, extra):
    vmem = pl.BlockSpec(memory_space=pltpu.VMEM)
    devices = operands[0].shape[0]
    blocks = jax.ShapeDtypeStruct((devices // 2, 2, rows, BLOCK), jnp.float32)
    mid = pltpu.VMEM((pairs, 2 * INNER, 2 * INNER), jnp.float32)
    return pl.pallas_call(
        kernel,
        in_specs=[pl.BlockSpec(memory_space=pltpu.SMEM)] + [vmem] * len(operands),
        out_specs=[pl.BlockSpec(memory_space=pl.ANY)] * 2,
        out_shape=[blocks, blocks],
        scratch_shapes=[mid] * (1 + extra)
        + [pltpu.VMEM((devices, 2, rows, BLOCK), jnp.float32), pltpu.SemaphoreType.DMA((devices,))],
        compiler_params=granted(16 + 8 * extra),
    )(place, *operands)


def azimuth_filter(place, early, late, fwd, inv, gain):
    operands = (early, late, fwd, inv, azimuth_twiddles(), gain)
    return filter_call(azimuth_kernel, place, operands, 2 * INNER, SLABS // 2, 1)


def narrow_filter(place, received, fwd, inv, wide):
    operands = (received, fwd, inv, *wide)
    return filter_call(narrow_kernel, place, operands, INNER, SLABS // 4, 0)


def pair_kernel(place_ref, keep_ref, other_ref, *out_refs):
    chip = place_ref[0] // 2
    for k, out_ref in enumerate(out_refs):
        block = jnp.bitwise_xor(chip, k)
        out_ref[...] = keep_ref[block] + other_ref[block]


def pair_add(place, keep, other):
    vmem = pl.BlockSpec(memory_space=pltpu.VMEM)
    chips, *block = keep.shape
    return pl.pallas_call(
        pair_kernel,
        in_specs=[pl.BlockSpec(memory_space=pltpu.SMEM), vmem, vmem],
        out_specs=[vmem] * chips,
        out_shape=[jax.ShapeDtypeStruct(tuple(block), jnp.float32)] * chips,
        name="pair_add",
        compiler_params=granted(8),
    )(place, keep, other)


def settle_kernel(*refs):
    total = refs[0][...]
    for ref in refs[1:-1]:
        total = total + ref[...]
    refs[-1][...] = total


def settle(parts):
    return pl.pallas_call(
        settle_kernel,
        out_shape=jax.ShapeDtypeStruct(parts[0].shape, jnp.float32),
        name="settle",
        compiler_params=granted(8),
    )(*parts)


def exact_dot(left, right):
    return jnp.dot(left, right, precision=lax.Precision.HIGHEST, preferred_element_type=jnp.float32)


def migrate_kernel(*refs):
    total = refs[0][...]
    for ref in refs[1:-2]:
        total = total + ref[...]
    refs[-1][...] = exact_dot(total.reshape(-1, BLOCK), refs[-2][0]).reshape(2, -1, BLOCK)


def migrate_last_kernel(a_ref, *refs):
    b_refs = refs[:-3]
    kernel_ref, o_ref = refs[-3], refs[-1]
    low = lax.broadcasted_iota(jnp.int32, (INNER, BLOCK), 1) < BLOCK // 2
    for part in range(2):
        first = a_ref[part]
        second = b_refs[0][part]
        for b_ref in b_refs[1:]:
            second = second + b_ref[part]
        rows = (
            jnp.where(low, first, pltpu.roll(second, BLOCK // 2, 1)),
            jnp.where(low, pltpu.roll(first, BLOCK // 2, 1), second),
        )
        for half in range(2):
            o_ref[part, half * INNER : (half + 1) * INNER, :] = exact_dot(rows[half], kernel_ref[0])


def migrate(block, kernel_body, parts, kernel, pulses, other=None):
    args = [*parts, kernel]
    in_specs = [pl.BlockSpec(part.shape, lambda i, n=part.ndim: (0,) * n) for part in parts]
    in_specs.append(pl.BlockSpec((1, BLOCK, BLOCK), lambda i: (block, 0, 0)))
    aliases = {}
    if other is not None:
        in_specs.append(pl.BlockSpec(memory_space=pl.ANY))
        aliases = {len(args): 0}
        args.append(other)
    return pl.pallas_call(
        kernel_body,
        grid=(1,),
        in_specs=in_specs,
        out_specs=pl.BlockSpec((2, pulses, BLOCK), lambda i: (0, 0, block)),
        out_shape=jax.ShapeDtypeStruct((2, pulses, 2 * BLOCK), jnp.float32),
        input_output_aliases=aliases,
        name="migrate",
        compiler_params=granted(8),
    )(*args)


def turn(blocks, axis):
    return lax.all_to_all(blocks, axis, split_axis=0, concat_axis=0, tiled=True)


def swap(block, distance):
    devices = range(lax.axis_size("chan"))
    return lax.ppermute(block, "chan", [(i, i ^ distance) for i in devices])


def body(echoes, chirp_phase, rcmc_kernel, rcmc_offset, az_phase, weight_table, weight_index):
    exact = lax.Precision.HIGHEST
    gates = echoes.shape[3]
    pulses = az_phase.shape[0]
    fwd_np, inv_np = inner_tables()
    fwd, inv = jnp.asarray(fwd_np), jnp.asarray(inv_np)
    devices = lax.axis_size("pulse")
    offsets = turn(jnp.broadcast_to(rcmc_offset, (devices, 1, rcmc_offset.shape[0])), "pulse")
    by_slab = chirp_phase.reshape(INNER, SLABS).T
    chirp = jnp.stack([jnp.cos(by_slab), jnp.sin(by_slab)]) * (1.0 / gates)
    tables = (fwd, inv, jnp.asarray(twiddles()), chirp)
    compressed = range_early(EARLY, echoes, tables)
    early = window_first(EARLY, offsets, compressed)
    late, compressed = range_late(EARLY, offsets, echoes, tables, compressed)
    part_a, part_b = window_second(offsets, compressed)

    table_count = weight_table.shape[1]
    entry_ids = lax.broadcasted_iota(jnp.int32, (weight_index.shape[1], table_count), 1)
    one_hot = (weight_index[0][:, None] == entry_ids).astype(jnp.float32)
    chosen = jnp.dot(weight_table, one_hot.T, precision=exact) * (1.0 / pulses)
    weights = jnp.repeat(chosen, DBLOCK, axis=1)
    phases = az_phase.T
    gain = jnp.stack(times(jnp.cos(phases), jnp.sin(phases), weights[0:1], weights[1:2]))
    gain = gain.reshape(2, 2, INNER, SLABS)

    early = turn(early, "pulse")
    late = turn(late, "pulse")
    part_a = turn(part_a, "pulse")
    part_b = turn(part_b, "pulse")
    place = lax.axis_index("chan").astype(jnp.int32).reshape(1)
    channels = lax.axis_size("chan")
    rows = pulses // channels
    wide = widen(gain[:, 1])
    keep, give = azimuth_filter(place, early, late, fwd, inv, gain[:, 0])
    first = pair_add(place, keep, swap(give, 1))
    first = [first[0]] + [swap(first[k], 2 * k) for k in range(1, channels // 2)]
    image = migrate(0, migrate_kernel, first, rcmc_kernel, rows)
    keep, give = narrow_filter(place, part_a, fwd, inv, wide)
    sum_a = pair_add(place, keep, swap(give, 1))
    sum_a = [sum_a[0]] + [swap(sum_a[k], 2 * k) for k in range(1, channels // 2)]
    sum_a = settle(sum_a)
    keep, give = narrow_filter(place, part_b, fwd, inv, wide)
    sum_b = pair_add(place, keep, swap(give, 1))
    sum_b = [sum_b[0]] + [swap(sum_b[k], 2 * k) for k in range(1, channels // 2)]
    return migrate(1, migrate_last_kernel, [sum_a, *sum_b], rcmc_kernel, rows, image)


def solution(mesh):
    return jax.shard_map(
        body,
        mesh=mesh,
        in_specs=(
            P("chan", None, "pulse", None),
            P(),
            P("pulse", None, None),
            P("pulse"),
            P(None, "pulse"),
            P(),
            P("chan", None),
        ),
        out_specs=P(None, "chan", "pulse"),
        check_vma=False,
    )
```

```python
import functools
import math

import jax
import jax.numpy as jnp
import numpy as np
from jax import lax
from jax.experimental import pallas as pl
from jax.experimental.pallas import tpu as pltpu
from jax.sharding import PartitionSpec as P

BLOCK = 128
DBLOCK = 128
SLABS = 32
INNER = 128
ROWS = 32
EARLY = 1


def granted(mebibytes):
    return pltpu.CompilerParams(vmem_limit_bytes=mebibytes * 2**20)


def split(values):
    high = values.astype(jnp.bfloat16)
    low = (values - high.astype(jnp.float32)).astype(jnp.bfloat16)
    return high, low


def dot(left, right):
    return jnp.dot(left, right, preferred_element_type=jnp.float32)


def dot3(left, right):
    return dot(left[0], right[0]) + dot(left[0], right[1]) + dot(left[1], right[0])


def inner_tables():
    index = np.arange(INNER)
    angles = 2.0 * math.pi / INNER * (index[:, None] * index[None, :] % INNER)
    table = np.block([[np.cos(angles), -np.sin(angles)], [np.sin(angles), np.cos(angles)]])
    bf16 = jnp.bfloat16.dtype
    high = table.astype(np.float32).astype(bf16)
    low = (table - high.astype(np.float64)).astype(np.float32).astype(bf16)
    return np.stack([high, low]), np.stack([high.T, low.T])


def twiddles():
    length = SLABS * INNER
    angles = 2.0 * math.pi / length * (np.arange(SLABS)[:, None] * np.arange(INNER)[None, :])
    return np.stack([np.cos(angles), -np.sin(angles)]).astype(np.float32)


def rotate(value, turn, length, sign):
    re, im = value
    if turn == 0:
        return value
    if 4 * turn == length:
        return (-im, re) if sign > 0 else (im, -re)
    half = math.sqrt(0.5)
    if 8 * turn == length:
        return ((re - im) * half, (re + im) * half) if sign > 0 else ((re + im) * half, (im - re) * half)
    if 8 * turn == 3 * length:
        return ((-re - im) * half, (re - im) * half) if sign > 0 else ((im - re) * half, (-re - im) * half)
    cosine = math.cos(2.0 * math.pi * turn / length)
    sine = sign * math.sin(2.0 * math.pi * turn / length)
    return re * cosine - im * sine, re * sine + im * cosine


def butterflies(values, sign):
    length = len(values)
    if length == 1:
        return values
    even = butterflies(values[0::2], sign)
    odd = butterflies(values[1::2], sign)
    lower, upper = [], []
    for turn in range(length // 2):
        er, ei = even[turn]
        tr, ti = rotate(odd[turn], turn, length, sign)
        lower.append((er + tr, ei + ti))
        upper.append((er - tr, ei - ti))
    return lower + upper


def times(re, im, cr, ci):
    return re * cr - im * ci, re * ci + im * cr


def compress(x_ref, fwd_ref, inv_ref, tw_ref, chirp_ref, mid_ref, y_ref):
    def first(tile, carry):
        rows = pl.ds(pl.multiple_of(tile * 8, 8), 8)
        values = [
            (x_ref[0, 0, rows, a * INNER : (a + 1) * INNER], x_ref[0, 1, rows, a * INNER : (a + 1) * INNER])
            for a in range(SLABS)
        ]
        for k, (re, im) in enumerate(butterflies(values, -1)):
            re, im = times(re, im, tw_ref[0, k : k + 1, :], tw_ref[1, k : k + 1, :])
            mid_ref[k, rows, :INNER] = re
            mid_ref[k, rows, INNER:] = im
        return carry

    lax.fori_loop(0, ROWS // 8, first, 0)

    group = 256 // ROWS
    chains = 2

    def middle(step, carry):
        spans = [pl.ds(pl.multiple_of((step * chains + c) * group, group), group) for c in range(chains)]
        spectra = [dot3(split(mid_ref[ks].reshape(256, 2 * INNER)), (fwd_ref[0], fwd_ref[1])) for ks in spans]
        for ks, spec in zip(spans, spectra):
            spec = spec.reshape(group, ROWS, 2 * INNER)
            cr = chirp_ref[0, ks, :].reshape(group, 1, INNER)
            ci = chirp_ref[1, ks, :].reshape(group, 1, INNER)
            re, im = times(spec[:, :, :INNER], spec[:, :, INNER:], cr, ci)
            filtered = jnp.concatenate([re, im], axis=2).reshape(256, 2 * INNER)
            back = dot3(split(filtered), (inv_ref[0], inv_ref[1])).reshape(group, ROWS, 2 * INNER)
            tr = tw_ref[0, ks, :].reshape(group, 1, INNER)
            ti = tw_ref[1, ks, :].reshape(group, 1, INNER)
            re, im = times(back[:, :, :INNER], back[:, :, INNER:], tr, -ti)
            mid_ref[ks, :, :INNER] = re
            mid_ref[ks, :, INNER:] = im
        return carry

    lax.fori_loop(0, SLABS // (group * chains), middle, 0)

    def last(tile, carry):
        rows = pl.ds(pl.multiple_of(tile * 8, 8), 8)
        lower = pl.ds(pl.multiple_of(ROWS + tile * 8, 8), 8)
        values = [(mid_ref[k, rows, :INNER], mid_ref[k, rows, INNER:]) for k in range(SLABS)]
        for a, (re, im) in enumerate(butterflies(values, 1)):
            y_ref[a, rows, :] = re
            y_ref[a, lower, :] = im
        return carry

    lax.fori_loop(0, ROWS // 8, last, 0)
    y_ref[SLABS] = jnp.zeros((2 * ROWS, INNER), jnp.float32)


def window_at(offset_ref, y_ref, dest, block, lanes):
    slab = 2 * dest + block
    back = INNER - offset_ref[dest, 0, block]
    here = pltpu.roll(y_ref[slab], back, 1)
    after = pltpu.roll(y_ref[slab + 1], back, 1)
    return jnp.where(lanes < back, here, after)


def first_windows(offset_ref, y_ref, z0_ref):
    lanes = lax.broadcasted_iota(jnp.int32, (2 * ROWS, INNER), 1)

    def window(step, carry):
        for part in range(4):
            dest = step * 4 + part
            z0_ref[dest, 0] = window_at(offset_ref, y_ref, dest, 0, lanes).reshape(2, ROWS, INNER)
        return carry

    lax.fori_loop(0, SLABS // 8, window, 0)


def second_windows(place_ref, offset_ref, y_ref, a_refs, zb_ref):
    lanes = lax.broadcasted_iota(jnp.int32, (2 * ROWS, INNER), 1)
    upper = pl.program_id(0) % 2
    mine = lanes // (INNER // 2) == upper

    for k, a_ref in enumerate(a_refs):
        dest = jnp.bitwise_xor(place_ref[0], k)
        gates = window_at(offset_ref, y_ref, dest, 1, lanes)
        other = pltpu.roll(gates, INNER // 2, 1)
        held = a_ref[...].reshape(2 * ROWS, INNER)
        a_ref[...] = jnp.where(mine, jnp.where(upper == 0, gates, other), held).reshape(2, ROWS, INNER)
        held = zb_ref[dest].reshape(2 * ROWS, INNER)
        zb_ref[dest] = jnp.where(mine, jnp.where(upper == 0, other, gates), held).reshape(2, ROWS, INNER)


def early_kernel(x_ref, fwd_ref, inv_ref, tw_ref, chirp_ref, y_ref, mid_ref):
    compress(x_ref, fwd_ref, inv_ref, tw_ref, chirp_ref, mid_ref, y_ref.at[0])


def first_kernel(offset_ref, y_ref, z0_ref):
    first_windows(offset_ref, y_ref.at[0], z0_ref)


def second_kernel(place_ref, offset_ref, y_ref, *refs):
    second_windows(place_ref, offset_ref, y_ref.at[0], refs[:-1], refs[-1])


def late_kernel(offset_ref, x_ref, fwd_ref, inv_ref, tw_ref, chirp_ref, other_ref, z0_ref, y_ref, mid_ref):
    compress(x_ref, fwd_ref, inv_ref, tw_ref, chirp_ref, mid_ref, y_ref.at[0])
    first_windows(offset_ref, y_ref.at[0], z0_ref)


def table_specs():
    whole = pl.BlockSpec((2, 2 * INNER, 2 * INNER), lambda i, *_: (0, 0, 0))
    table = pl.BlockSpec((2, SLABS, INNER), lambda i, *_: (0, 0, 0))
    return [whole, whole, table, table]


def echo_spec(start, gates):
    return pl.BlockSpec((1, 2, ROWS, gates), lambda i, *_: (0, 0, (i % 2) * (INNER // ROWS) + start + i // 2, 0))


def compressed_shape(echoes):
    return jax.ShapeDtypeStruct((echoes.shape[2] // ROWS, SLABS + 1, 2 * ROWS, INNER), jnp.float32)


def compressed_spec(start):
    return pl.BlockSpec((1, SLABS + 1, 2 * ROWS, INNER), lambda i, *_: (2 * start + i, 0, 0, 0))


def range_early(tiles, echoes, tables):
    return pl.pallas_call(
        early_kernel,
        grid=(2 * tiles,),
        in_specs=[echo_spec(0, echoes.shape[3])] + table_specs(),
        out_specs=compressed_spec(0),
        out_shape=compressed_shape(echoes),
        scratch_shapes=[pltpu.VMEM((SLABS, ROWS, 2 * INNER), jnp.float32)],
        name="range_early",
    )(echoes, *tables)


def first_shape(tiles):
    return jax.ShapeDtypeStruct((SLABS // 2, 2, 2, tiles * ROWS, BLOCK), jnp.float32)


def first_spec():
    return pl.BlockSpec((SLABS // 2, 1, 2, ROWS, BLOCK), lambda i, *_: (0, i % 2, 0, i // 2, 0))


def window_first(tiles, offsets, compressed):
    return pl.pallas_call(
        first_kernel,
        grid_spec=pltpu.PrefetchScalarGridSpec(
            num_scalar_prefetch=1, grid=(2 * tiles,), in_specs=[compressed_spec(0)], out_specs=first_spec()
        ),
        out_shape=first_shape(tiles),
        name="window_first",
    )(offsets, compressed)


def range_late(start, offsets, echoes, tables, compressed):
    tiles = INNER // ROWS - start
    return pl.pallas_call(
        late_kernel,
        grid_spec=pltpu.PrefetchScalarGridSpec(
            num_scalar_prefetch=1,
            grid=(2 * tiles,),
            in_specs=[echo_spec(start, echoes.shape[3])] + table_specs() + [pl.BlockSpec(memory_space=pl.ANY)],
            out_specs=[first_spec(), compressed_spec(start)],
            scratch_shapes=[pltpu.VMEM((SLABS, ROWS, 2 * INNER), jnp.float32)],
        ),
        out_shape=[first_shape(tiles), compressed_shape(echoes)],
        input_output_aliases={6: 1},
        name="range_late",
    )(offsets, echoes, *tables, compressed)


def window_second(place, offsets, compressed):
    dests = SLABS // 2
    piece = jax.ShapeDtypeStruct((2, INNER, BLOCK), jnp.float32)
    part = jax.ShapeDtypeStruct((dests, 2, INNER, BLOCK), jnp.float32)
    piece_spec = pl.BlockSpec((2, ROWS, BLOCK), lambda i, *_: (0, i // 2, 0))
    part_spec = pl.BlockSpec((dests, 2, ROWS, BLOCK), lambda i, *_: (0, 0, i // 2, 0))
    return pl.pallas_call(
        second_kernel,
        grid_spec=pltpu.PrefetchScalarGridSpec(
            num_scalar_prefetch=2,
            grid=(compressed.shape[0],),
            in_specs=[compressed_spec(0)],
            out_specs=[piece_spec] * dests + [part_spec],
        ),
        out_shape=[piece] * dests + [part],
        name="window_second",
    )(place, offsets, compressed)


def hand_out(place_ref, o_ref, keep_ref, give_ref, sem):
    core = jnp.bitwise_and(place_ref[0], 1)
    copies = []
    for block in range(o_ref.shape[0]):
        source = o_ref.at[jnp.bitwise_xor(core, block)]
        target = (keep_ref, give_ref)[block % 2].at[block // 2]
        copies.append(pltpu.make_async_copy(source, target, sem.at[block]))
    for copy in copies:
        copy.start()
    for copy in copies:
        copy.wait()


def azimuth_kernel(place_ref, early_ref, late_ref, fwd_ref, inv_ref, tw_ref, gain_ref, keep_ref, give_ref, mid_ref, wide_ref, o_ref, sem):
    edge = early_ref.shape[3] // 8

    def first(x_ref, base, tile, carry):
        start = pl.multiple_of(tile * 8, 8)
        rows = pl.ds(start, 8)
        lower = pl.ds(pl.multiple_of(INNER + tile * 8, 8), 8)
        here = pl.ds(pl.multiple_of((tile - base) * 8, 8), 8)
        values = [(x_ref[a // 2, a % 2, 0, here, :], x_ref[a // 2, a % 2, 1, here, :]) for a in range(SLABS)]
        tr, ti = tw_ref[0, rows, :], tw_ref[1, rows, :]
        gr, gi = gain_ref[0, rows, :], gain_ref[1, rows, :]
        for k, (re, im) in enumerate(butterflies(values, -1)):
            re, im = times(re, im, tr[:, k : k + 1], ti[:, k : k + 1])
            lane = slice((k % 2) * INNER, (k % 2 + 1) * INNER)
            mid_ref[k // 2, rows, lane] = re
            mid_ref[k // 2, lower, lane] = im
            wide_ref[k // 2, rows, lane] = jnp.broadcast_to(gr[:, k : k + 1], (8, INNER))
            wide_ref[k // 2, lower, lane] = jnp.broadcast_to(gi[:, k : k + 1], (8, INNER))
        return carry

    lax.fori_loop(0, edge, functools.partial(first, early_ref, 0), 0)
    lax.fori_loop(edge, INNER // 8, functools.partial(first, late_ref, edge), 0)

    def middle(step, carry):
        pairs = [2 * step, 2 * step + 1]
        spectra = [dot3((inv_ref[0], inv_ref[1]), split(mid_ref[pair])) for pair in pairs]
        for pair, spec in zip(pairs, spectra):
            re, im = times(spec[:INNER], spec[INNER:], wide_ref[pair, :INNER, :], wide_ref[pair, INNER:, :])
            mid_ref[pair] = dot3((fwd_ref[0], fwd_ref[1]), split(jnp.concatenate([re, im], axis=0)))
        return carry

    lax.fori_loop(0, SLABS // 4, middle, 0)

    def last(tile, carry):
        rows = pl.ds(pl.multiple_of(tile * 8, 8), 8)
        lower = pl.ds(pl.multiple_of(INNER + tile * 8, 8), 8)
        halves = (rows, lower)
        tr, ti = tw_ref[0, rows, :], tw_ref[1, rows, :]
        values = []
        for k in range(SLABS):
            lane = slice((k % 2) * INNER, (k % 2 + 1) * INNER)
            re, im = mid_ref[k // 2, rows, lane], mid_ref[k // 2, lower, lane]
            values.append(times(re, im, tr[:, k : k + 1], -ti[:, k : k + 1]))
        for a, (re, im) in enumerate(butterflies(values, 1)):
            o_ref[a // 2, 0, halves[a % 2], :] = re
            o_ref[a // 2, 1, halves[a % 2], :] = im
        return carry

    lax.fori_loop(0, INNER // 8, last, 0)

    hand_out(place_ref, o_ref, keep_ref, give_ref, sem)


def narrow_kernel(place_ref, x_ref, fwd_ref, inv_ref, tw_ref, gain_ref, keep_ref, give_ref, mid_ref, o_ref, sem):
    half = SLABS // 2
    high = lax.broadcasted_iota(jnp.int32, (8, INNER), 1) >= INNER // 2
    sign = jnp.where(high, -1.0, 1.0)

    def turned(re, im, k, direction):
        cosine = math.cos(2.0 * math.pi * k / SLABS)
        sine = direction * math.sin(2.0 * math.pi * k / SLABS)
        return times(re, im, jnp.where(high, cosine, 1.0), jnp.where(high, sine, 0.0))

    def crossed(value):
        return pltpu.roll(value, INNER // 2, 1) + sign * value

    def place_of(k):
        return k // 2, slice((k % 2) * INNER, (k % 2 + 1) * INNER)

    def first(tile, carry):
        rows = pl.ds(pl.multiple_of(tile * 8, 8), 8)
        lower = pl.ds(pl.multiple_of(INNER + tile * 8, 8), 8)
        values = [(x_ref[i, 0, rows, :], x_ref[i, 1, rows, :]) for i in range(half)]
        for k, (re, im) in enumerate(butterflies(values, -1)):
            pair, lane = place_of(k)
            re, im = turned(re, im, k, -1)
            re, im = times(crossed(re), crossed(im), tw_ref[pair, rows, lane], tw_ref[pair, lower, lane])
            mid_ref[pair, rows, lane] = re
            mid_ref[pair, lower, lane] = im
        return carry

    lax.fori_loop(0, INNER // 8, first, 0, unroll=2)

    def middle(step, carry):
        pairs = [2 * step, 2 * step + 1]
        spectra = [dot3((inv_ref[0], inv_ref[1]), split(mid_ref[pair])) for pair in pairs]
        for pair, spec in zip(pairs, spectra):
            re, im = times(spec[:INNER], spec[INNER:], gain_ref[pair, :INNER, :], gain_ref[pair, INNER:, :])
            mid_ref[pair] = dot3((fwd_ref[0], fwd_ref[1]), split(jnp.concatenate([re, im], axis=0)))
        return carry

    lax.fori_loop(0, half // 4, middle, 0)

    def last(tile, carry):
        rows = pl.ds(pl.multiple_of(tile * 8, 8), 8)
        lower = pl.ds(pl.multiple_of(INNER + tile * 8, 8), 8)
        values = []
        for k in range(half):
            pair, lane = place_of(k)
            re, im = times(
                mid_ref[pair, rows, lane], mid_ref[pair, lower, lane], tw_ref[pair, rows, lane], -tw_ref[pair, lower, lane]
            )
            values.append(turned(crossed(re), crossed(im), k, 1))
        for i, (re, im) in enumerate(butterflies(values, 1)):
            o_ref[i, 0, rows, :] = re
            o_ref[i, 1, rows, :] = im
        return carry

    lax.fori_loop(0, INNER // 8, last, 0, unroll=2)
    hand_out(place_ref, o_ref, keep_ref, give_ref, sem)


def pieces_kernel(place_ref, from_ref, *refs):
    pieces = refs[: SLABS // 2]
    *rest, x_ref, loads = refs[SLABS // 2 :]
    copies = [
        pltpu.make_async_copy(piece, x_ref.at[jnp.bitwise_xor(from_ref[0], k)], loads.at[k]) for k, piece in enumerate(pieces)
    ]
    for copy in copies:
        copy.start()
    for copy in copies:
        copy.wait()
    narrow_kernel(place_ref, x_ref, *rest)


def widen_kernel(tw_ref, gain_ref, tw_wide_ref, gain_wide_ref):
    half = SLABS // 2
    high = lax.broadcasted_iota(jnp.int32, (8, INNER), 1) >= INNER // 2

    def spread(tile, carry):
        rows = pl.ds(pl.multiple_of(tile * 8, 8), 8)
        for source, target in ((tw_ref, tw_wide_ref), (gain_ref, gain_wide_ref)):
            for part in range(2):
                value = source[part, rows, :]
                where = pl.ds(pl.multiple_of(part * INNER + tile * 8, 8), 8)
                for k in range(half):
                    lane = slice((k % 2) * INNER, (k % 2 + 1) * INNER)
                    target[k // 2, where, lane] = jnp.where(high, value[:, k + half : k + half + 1], value[:, k : k + 1])
        return carry

    lax.fori_loop(0, INNER // 8, spread, 0)


def azimuth_twiddles():
    return jnp.asarray(twiddles().transpose(0, 2, 1))


def widen(gain):
    wide = jax.ShapeDtypeStruct((SLABS // 4, 2 * INNER, 2 * INNER), jnp.float32)
    return pl.pallas_call(widen_kernel, out_shape=[wide, wide], name="widen", compiler_params=granted(8))(azimuth_twiddles(), gain)


def filter_call(kernel, place, operands, rows, pairs, extra):
    vmem = pl.BlockSpec(memory_space=pltpu.VMEM)
    devices = operands[0].shape[0]
    blocks = jax.ShapeDtypeStruct((devices // 2, 2, rows, BLOCK), jnp.float32)
    mid = pltpu.VMEM((pairs, 2 * INNER, 2 * INNER), jnp.float32)
    return pl.pallas_call(
        kernel,
        in_specs=[pl.BlockSpec(memory_space=pltpu.SMEM)] + [vmem] * len(operands),
        out_specs=[pl.BlockSpec(memory_space=pl.ANY)] * 2,
        out_shape=[blocks, blocks],
        scratch_shapes=[mid] * (1 + extra)
        + [pltpu.VMEM((devices, 2, rows, BLOCK), jnp.float32), pltpu.SemaphoreType.DMA((devices,))],
        compiler_params=granted(16 + 8 * extra),
    )(place, *operands)


def azimuth_filter(place, early, late, fwd, inv, gain):
    operands = (early, late, fwd, inv, azimuth_twiddles(), gain)
    return filter_call(azimuth_kernel, place, operands, 2 * INNER, SLABS // 2, 1)


def narrow_filter(place, received, fwd, inv, wide):
    operands = (received, fwd, inv, *wide)
    return filter_call(narrow_kernel, place, operands, INNER, SLABS // 4, 0)


def pieces_filter(place, source, pieces, fwd, inv, wide):
    vmem, smem = pl.BlockSpec(memory_space=pltpu.VMEM), pl.BlockSpec(memory_space=pltpu.SMEM)
    devices = len(pieces)
    blocks = jax.ShapeDtypeStruct((devices // 2, 2, INNER, BLOCK), jnp.float32)
    whole = pltpu.VMEM((devices, 2, INNER, BLOCK), jnp.float32)
    return pl.pallas_call(
        pieces_kernel,
        in_specs=[smem, smem] + [pl.BlockSpec(memory_space=pl.ANY)] * devices + [vmem] * 4,
        out_specs=[pl.BlockSpec(memory_space=pl.ANY)] * 2,
        out_shape=[blocks, blocks],
        scratch_shapes=[
            pltpu.VMEM((SLABS // 4, 2 * INNER, 2 * INNER), jnp.float32),
            whole,
            pltpu.SemaphoreType.DMA((devices,)),
            whole,
            pltpu.SemaphoreType.DMA((devices,)),
        ],
        name="pieces_filter",
        compiler_params=granted(18),
    )(place, source, *pieces, fwd, inv, *wide)


def pair_kernel(place_ref, keep_ref, other_ref, *out_refs):
    chip = place_ref[0] // 2
    for k, out_ref in enumerate(out_refs):
        block = jnp.bitwise_xor(chip, k)
        out_ref[...] = keep_ref[block] + other_ref[block]


def pair_add(place, keep, other):
    vmem = pl.BlockSpec(memory_space=pltpu.VMEM)
    chips, *block = keep.shape
    return pl.pallas_call(
        pair_kernel,
        in_specs=[pl.BlockSpec(memory_space=pltpu.SMEM), vmem, vmem],
        out_specs=[vmem] * chips,
        out_shape=[jax.ShapeDtypeStruct(tuple(block), jnp.float32)] * chips,
        name="pair_add",
        compiler_params=granted(8),
    )(place, keep, other)


def settle_kernel(*refs):
    total = refs[0][...]
    for ref in refs[1:-1]:
        total = total + ref[...]
    refs[-1][...] = total


def settle(parts):
    return pl.pallas_call(
        settle_kernel,
        out_shape=jax.ShapeDtypeStruct(parts[0].shape, jnp.float32),
        name="settle",
        compiler_params=granted(8),
    )(*parts)


def exact_dot(left, right):
    return jnp.dot(left, right, precision=lax.Precision.HIGHEST, preferred_element_type=jnp.float32)


def migrate_kernel(*refs):
    total = refs[0][...]
    for ref in refs[1:-2]:
        total = total + ref[...]
    refs[-1][...] = exact_dot(total.reshape(-1, BLOCK), refs[-2][0]).reshape(2, -1, BLOCK)


def migrate_last_kernel(a_ref, *refs):
    b_refs = refs[:-3]
    kernel_ref, o_ref = refs[-3], refs[-1]
    low = lax.broadcasted_iota(jnp.int32, (INNER, BLOCK), 1) < BLOCK // 2
    for part in range(2):
        first = a_ref[part]
        second = b_refs[0][part]
        for b_ref in b_refs[1:]:
            second = second + b_ref[part]
        rows = (
            jnp.where(low, first, pltpu.roll(second, BLOCK // 2, 1)),
            jnp.where(low, pltpu.roll(first, BLOCK // 2, 1), second),
        )
        for half in range(2):
            o_ref[part, half * INNER : (half + 1) * INNER, :] = exact_dot(rows[half], kernel_ref[0])


def migrate(block, kernel_body, parts, kernel, pulses, other=None):
    args = [*parts, kernel]
    in_specs = [pl.BlockSpec(part.shape, lambda i, n=part.ndim: (0,) * n) for part in parts]
    in_specs.append(pl.BlockSpec((1, BLOCK, BLOCK), lambda i: (block, 0, 0)))
    aliases = {}
    if other is not None:
        in_specs.append(pl.BlockSpec(memory_space=pl.ANY))
        aliases = {len(args): 0}
        args.append(other)
    return pl.pallas_call(
        kernel_body,
        grid=(1,),
        in_specs=in_specs,
        out_specs=pl.BlockSpec((2, pulses, BLOCK), lambda i: (0, 0, block)),
        out_shape=jax.ShapeDtypeStruct((2, pulses, 2 * BLOCK), jnp.float32),
        input_output_aliases=aliases,
        name="migrate",
        compiler_params=granted(8),
    )(*args)


def turn(blocks, axis):
    return lax.all_to_all(blocks, axis, split_axis=0, concat_axis=0, tiled=True)


def swap(block, distance, axis="chan"):
    return lax.ppermute(block, axis, [(i, i ^ distance) for i in range(lax.axis_size(axis))])


def body(echoes, chirp_phase, rcmc_kernel, rcmc_offset, az_phase, weight_table, weight_index):
    exact = lax.Precision.HIGHEST
    gates = echoes.shape[3]
    pulses = az_phase.shape[0]
    fwd_np, inv_np = inner_tables()
    fwd, inv = jnp.asarray(fwd_np), jnp.asarray(inv_np)
    devices = lax.axis_size("pulse")
    offsets = turn(jnp.broadcast_to(rcmc_offset, (devices, 1, rcmc_offset.shape[0])), "pulse")
    by_slab = chirp_phase.reshape(INNER, SLABS).T
    chirp = jnp.stack([jnp.cos(by_slab), jnp.sin(by_slab)]) * (1.0 / gates)
    tables = (fwd, inv, jnp.asarray(twiddles()), chirp)
    compressed = range_early(EARLY, echoes, tables)
    early = window_first(EARLY, offsets, compressed)
    late, compressed = range_late(EARLY, offsets, echoes, tables, compressed)
    source = lax.axis_index("pulse").astype(jnp.int32).reshape(1)
    *part_a, part_b = window_second(source, offsets, compressed)

    table_count = weight_table.shape[1]
    entry_ids = lax.broadcasted_iota(jnp.int32, (weight_index.shape[1], table_count), 1)
    one_hot = (weight_index[0][:, None] == entry_ids).astype(jnp.float32)
    chosen = jnp.dot(weight_table, one_hot.T, precision=exact) * (1.0 / pulses)
    weights = jnp.repeat(chosen, DBLOCK, axis=1)
    phases = az_phase.T
    gain = jnp.stack(times(jnp.cos(phases), jnp.sin(phases), weights[0:1], weights[1:2]))
    gain = gain.reshape(2, 2, INNER, SLABS)

    early = turn(early, "pulse")
    late = turn(late, "pulse")
    part_a = [part_a[0]] + [swap(part_a[k], k, "pulse") for k in range(1, devices)]
    part_b = turn(part_b, "pulse")
    place = lax.axis_index("chan").astype(jnp.int32).reshape(1)
    channels = lax.axis_size("chan")
    rows = pulses // channels
    wide = widen(gain[:, 1])
    keep, give = azimuth_filter(place, early, late, fwd, inv, gain[:, 0])
    first = pair_add(place, keep, swap(give, 1))
    first = [first[0]] + [swap(first[k], 2 * k) for k in range(1, channels // 2)]
    image = migrate(0, migrate_kernel, first, rcmc_kernel, rows)
    keep, give = pieces_filter(place, source, part_a, fwd, inv, wide)
    sum_a = pair_add(place, keep, swap(give, 1))
    sum_a = [sum_a[0]] + [swap(sum_a[k], 2 * k) for k in range(1, channels // 2)]
    sum_a = settle(sum_a)
    keep, give = narrow_filter(place, part_b, fwd, inv, wide)
    sum_b = pair_add(place, keep, swap(give, 1))
    sum_b = [sum_b[0]] + [swap(sum_b[k], 2 * k) for k in range(1, channels // 2)]
    return migrate(1, migrate_last_kernel, [sum_a, *sum_b], rcmc_kernel, rows, image)


def solution(mesh):
    return jax.shard_map(
        body,
        mesh=mesh,
        in_specs=(
            P("chan", None, "pulse", None),
            P(),
            P("pulse", None, None),
            P("pulse"),
            P(None, "pulse"),
            P(),
            P("chan", None),
        ),
        out_specs=P(None, "chan", "pulse"),
        check_vma=False,
    )
```
